32 devices in a mesh: dp: 8 (over z, x), obj: 4 (over y, core).
Axes of the slice: x: 2, y: 2, z: 4, core: 2. Of those that a mesh axis runs over, the one named last changes fastest.
Arguments:
- object_field: float32 [2, 2048, 2048], P(None, 'dp', 'obj'), may hold values from -6 to 6
- probe_modes: float32 [4, 2, 256, 256], replicated, may hold values from -3 to 3
- amplitude: float32 [192, 256, 256], P(('dp', 'obj')), may hold values from 0.3 to 5
- offsets: int32 [192, 2], P(('dp', 'obj')), may hold values from -128 to 1919, as said below
Outputs:
- object_out: float32 [2, 2048, 2048], P(None, 'dp', 'obj')
- probe_out: float32 [4, 2, 256, 256], replicated
The draws below stay inside these ranges and needn't reach their ends.
Inputs may be any that keep to these rules, and one draw needn't show every extreme that they name: `offsets`: the position in slot n of a device's 6 slots has its patch centre (offset plus 256 / 2 in both coordinates) inside that device's tile of 256 x 512 object pixels; on every device one position's centre is the tile's first pixel and one is its last pixel.
All inputs are finite; a program needn't handle non-finite values.
Results may differ from the reference program's by a relative error of at most 0.003.
Values may be sent and summed in bfloat16 or wider, within the bound.
No kernel may reach another device: no remote copies, remote signals or barrier semaphores. Data moves between devices by JAX's collectives and lax.ppermute only.
A program may use at most 128 MiB of HBM per device.

```python
import math
import jax
import jax.numpy as jnp
from jax import lax

P_SIZE = 256
MODES = 4
TY = 256
TX = 512
POS_DEV = 6
ITERS = 2
OY = 2048
OX = 2048
POS = 192


def draw_offsets(key, part):
    key_rows = jax.random.fold_in(key, 11)
    key_cols = jax.random.fold_in(key, 23)
    key_turn = jax.random.fold_in(key, 37)
    slot_ids = jnp.arange(POS, dtype=jnp.int32)
    device_ids = slot_ids // POS_DEV
    across_count = OX // TX
    tile_row = device_ids // across_count
    tile_col = device_ids % across_count
    row_pick = jax.random.randint(key_rows, (POS,), 0, TY, dtype=jnp.int32)
    col_pick = jax.random.randint(key_cols, (POS,), 0, TX, dtype=jnp.int32)
    rotate_by = jax.random.randint(key_turn, (POS // POS_DEV,), 0, POS_DEV, dtype=jnp.int32)
    local_slot = (slot_ids % POS_DEV + rotate_by[device_ids]) % POS_DEV
    row_pick = jnp.where(local_slot == 0, 0, jnp.where(local_slot == 1, TY - 1, row_pick))
    col_pick = jnp.where(local_slot == 0, 0, jnp.where(local_slot == 1, TX - 1, col_pick))
    half = P_SIZE // 2
    row_first = tile_row * TY + row_pick - half
    col_first = tile_col * TX + col_pick - half
    return jnp.stack([row_first, col_first], axis=1).astype(jnp.int32)


def levels(own_key, shape, cuts, least, largest):
    loudness, own = 1.0, jax.random.fold_in(own_key, 6)
    for dim, blocks in cuts:
        draws = jnp.exp(jax.random.uniform(jax.random.fold_in(own, dim), (blocks,), jnp.float32, least / len(cuts), largest / len(cuts)))
        loudness = loudness * jnp.repeat(draws, shape[dim] // blocks).reshape([-1 if axis == dim else 1 for axis in range(len(shape))])
    return loudness


def centred(rng, extent, deviation, bound, split=(), kind=jnp.bfloat16):
    values = jax.random.normal(rng, extent, jnp.float32) * deviation
    if len(split) > 0:
        values = levels(rng, extent, split, -0.22, 0.18) * values
    return jnp.clip(values, min=-bound, max=bound).astype(kind)


def setup_inputs(seed: int = 0) -> dict:
    streams_of = jax.random.split(jax.random.key(seed), 5)
    object_field = centred(streams_of[0], (2, OY, OX), 1.0, 6.0, ((1, 8), (2, 4)), jnp.float32)
    probe_modes = centred(streams_of[1], (MODES, 2, P_SIZE, P_SIZE), 0.5, 3.0, (), jnp.float32)
    amplitude = jnp.clip(jnp.exp(math.log(5.0) - 2.8134107 * jax.random.uniform(streams_of[2], (POS, P_SIZE, P_SIZE), jnp.float32) ** levels(streams_of[2], (POS, P_SIZE, P_SIZE), ((0, 32),), -0.2, 0.2)), 0.3, 5.0)
    offsets = draw_offsets(jax.random.fold_in(streams_of[4], 71), 0)
    return {"object_field": object_field, "probe_modes": probe_modes, "amplitude": amplitude, "offsets": offsets}


EPSILON = 1e-06

def dft_tables(length):
    counter = jnp.arange(length, dtype=jnp.int32)
    phase_steps = counter[:, None] * counter[None, :] % length
    angle_grid = phase_steps.astype(jnp.float32) * (2.0 * jnp.pi / length)
    norm_factor = 1.0 / jnp.sqrt(jnp.float32(length))
    real_table = (jnp.cos(angle_grid) * norm_factor).astype(jnp.bfloat16)
    imag_table = (-jnp.sin(angle_grid) * norm_factor).astype(jnp.bfloat16)
    return (real_table, imag_table)

def propagate(patches, probe_low, amplitude_block, real_table, imag_table):
    table_re = real_table.astype(jnp.float32)
    table_im = imag_table.astype(jnp.float32)
    patch_re = patches[:, 0].astype(jnp.float32)[:, None]
    patch_im = patches[:, 1].astype(jnp.float32)[:, None]
    probe_re = probe_low[:, 0].astype(jnp.float32)[None]
    probe_im = probe_low[:, 1].astype(jnp.float32)[None]
    wave_re = (probe_re * patch_re - probe_im * patch_im).astype(jnp.bfloat16).astype(jnp.float32)
    wave_im = (probe_re * patch_im + probe_im * patch_re).astype(jnp.bfloat16).astype(jnp.float32)
    half_re = jnp.einsum('kr,bmrc->bmkc', table_re, wave_re) - jnp.einsum('kr,bmrc->bmkc', table_im, wave_im)
    half_im = jnp.einsum('kr,bmrc->bmkc', table_re, wave_im) + jnp.einsum('kr,bmrc->bmkc', table_im, wave_re)
    half_re = half_re.astype(jnp.bfloat16).astype(jnp.float32)
    half_im = half_im.astype(jnp.bfloat16).astype(jnp.float32)
    far_re = jnp.einsum('bmrc,ck->bmrk', half_re, table_re) - jnp.einsum('bmrc,ck->bmrk', half_im, table_im)
    far_im = jnp.einsum('bmrc,ck->bmrk', half_re, table_im) + jnp.einsum('bmrc,ck->bmrk', half_im, table_re)
    intensity = lax.optimization_barrier(jnp.sum(far_re * far_re + far_im * far_im, axis=1))
    ratio = amplitude_block / jnp.maximum(jnp.sqrt(intensity), 1.0) - 1.0
    diff_re = (far_re * ratio[:, None]).astype(jnp.bfloat16).astype(jnp.float32)
    diff_im = (far_im * ratio[:, None]).astype(jnp.bfloat16).astype(jnp.float32)
    back_re = jnp.einsum('kr,bmrc->bmkc', table_re, diff_re) + jnp.einsum('kr,bmrc->bmkc', table_im, diff_im)
    back_im = jnp.einsum('kr,bmrc->bmkc', table_re, diff_im) - jnp.einsum('kr,bmrc->bmkc', table_im, diff_re)
    back_re = back_re.astype(jnp.bfloat16).astype(jnp.float32)
    back_im = back_im.astype(jnp.bfloat16).astype(jnp.float32)
    chi_re = jnp.einsum('bmrc,ck->bmrk', back_re, table_re) + jnp.einsum('bmrc,ck->bmrk', back_im, table_im)
    chi_im = jnp.einsum('bmrc,ck->bmrk', back_im, table_re) - jnp.einsum('bmrc,ck->bmrk', back_re, table_im)
    object_re = lax.optimization_barrier(jnp.sum(probe_re * chi_re + probe_im * chi_im, axis=1))
    object_im = lax.optimization_barrier(jnp.sum(probe_re * chi_im - probe_im * chi_re, axis=1))
    probe_re_grad = lax.optimization_barrier(jnp.sum(patch_re * chi_re + patch_im * chi_im, axis=0))
    probe_im_grad = lax.optimization_barrier(jnp.sum(patch_re * chi_im - patch_im * chi_re, axis=0))
    return (jnp.stack([object_re, object_im], axis=1), jnp.stack([probe_re_grad, probe_im_grad], axis=1))

def reference(object_field, probe_modes, amplitude, offsets):
    half = P_SIZE // 2
    real_table, imag_table = dft_tables(P_SIZE)
    top_rows = (offsets[:, 0] + half).astype(jnp.int32)
    left_cols = (offsets[:, 1] + half).astype(jnp.int32)
    zero_index = jnp.zeros((), jnp.int32)
    current = object_field
    probe = probe_modes
    block_count = POS // POS_DEV
    for turn in range(ITERS):
        object_low = current.astype(jnp.bfloat16)
        padded = jnp.pad(object_low, ((0, 0), (half, half), (half, half)))
        probe_low = probe.astype(jnp.bfloat16)
        power = lax.optimization_barrier(jnp.sum(probe_low.astype(jnp.float32) ** 2, axis=(0, 1)))
        object_scale = 1.0 / (jnp.max(power) + EPSILON)

        def block_step(carry, block_index):
            grad_pad, probe_grad = carry
            start = (block_index * POS_DEV).astype(jnp.int32)
            rows = lax.dynamic_slice_in_dim(top_rows, start, POS_DEV)
            cols = lax.dynamic_slice_in_dim(left_cols, start, POS_DEV)
            amps = lax.dynamic_slice_in_dim(amplitude, start, POS_DEV, 0)
            patches = jax.vmap(lambda row, col: lax.dynamic_slice(padded, (zero_index, row, col), (2, P_SIZE, P_SIZE)))(rows, cols)
            object_terms, probe_terms = propagate(patches, probe_low, amps, real_table, imag_table)

            def add_one(position, grid):
                row = rows[position]
                col = cols[position]
                window = lax.dynamic_slice(grid, (zero_index, row, col), (2, P_SIZE, P_SIZE))
                return lax.dynamic_update_slice(grid, window + object_terms[position], (zero_index, row, col))
            grad_pad = lax.fori_loop(0, POS_DEV, add_one, grad_pad)
            return ((grad_pad, probe_grad + probe_terms), None)
        start_grad = jnp.zeros((2, OY + P_SIZE, OX + P_SIZE), jnp.float32)
        start_probe = jnp.zeros((MODES, 2, P_SIZE, P_SIZE), jnp.float32)
        (grad_pad, probe_grad), unused = lax.scan(block_step, (start_grad, start_probe), jnp.arange(block_count, dtype=jnp.int32))
        current = current + grad_pad[:, half:half + OY, half:half + OX] * object_scale
        probe = probe + probe_grad / POS
    return (current, probe)
```

```python
import jax
import jax.numpy as jnp
from jax import lax
from jax.experimental import pallas as pl
from jax.experimental.pallas import tpu as pltpu
from jax.sharding import PartitionSpec as P


ITERS = 2


EPSILON = 1e-06


LANES = 128


def swap_bit(values, axis, bit):
    return lax.ppermute(values, axis, [(i, i ^ bit) for i in range(lax.axis_size(axis))])


def neighbours(before, after, axis):
    count = lax.axis_size(axis)
    odd = lax.axis_index(axis) % 2 == 1
    inner = [(i, i ^ 1) for i in range(count)]
    outer = [(i, i + 1) for i in range(1, count - 1, 2)]
    outer = outer + [(target, source) for source, target in outer]
    from_outer = lax.ppermute(jnp.where(odd, after, before), axis, outer)
    from_inner = lax.ppermute(jnp.where(odd, before, after), axis, inner)
    previous = jnp.where(odd, from_inner, from_outer)
    following = jnp.where(odd, from_outer, from_inner)
    return previous, following


def dft_tables(length):
    counter = jnp.arange(length, dtype=jnp.int32)
    phase_steps = counter[:, None] * counter[None, :] % length
    angle_grid = phase_steps.astype(jnp.float32) * (2.0 * jnp.pi / length)
    norm_factor = 1.0 / jnp.sqrt(jnp.float32(length))
    real_table = (jnp.cos(angle_grid) * norm_factor).astype(jnp.bfloat16)
    imag_table = (-jnp.sin(angle_grid) * norm_factor).astype(jnp.bfloat16)
    return (real_table, imag_table)


def split_tables(length):
    real_table, imag_table = dft_tables(length)
    half = length // 2
    lefts = []
    for first in (0, 1):
        re = real_table[first::2, :half]
        im = imag_table[first::2, :half]
        lefts.append(
            jnp.concatenate(
                [jnp.concatenate([re, -im], axis=1), jnp.concatenate([im, re], axis=1)], axis=0
            )
        )
    return jnp.stack(lefts + [lefts[0].T, lefts[1].T])


def even_odd(values):
    side = values.shape[-1]
    order = jnp.concatenate([jnp.arange(0, side, 2), jnp.arange(1, side, 2)])
    pick = (jnp.arange(side)[:, None] == order[None, :]).astype(jnp.float32)
    right = jnp.einsum(
        "brc,ck->brk", values, pick, precision=lax.Precision.HIGHEST,
        preferred_element_type=jnp.float32,
    )
    return jnp.einsum(
        "rk,brc->bkc", pick, right, precision=lax.Precision.HIGHEST,
        preferred_element_type=jnp.float32,
    )


def mm(left, right):
    return jnp.dot(left, right, preferred_element_type=jnp.float32)


def propagate_body(
    rows_ref, cols_ref, tile_ref, above_ref, below_ref, left_ref, right_ref, probe_ref, amp_ref,
    table_ref, grad_ref, rim_ref, probe_grad_ref, ext_f32, patch_ref, far_ref, acc_ref, scale_ref,
):
    modes = probe_ref.shape[0]
    side = probe_ref.shape[2]
    half = side // 2
    step = pl.program_id(0)
    tiles = ext_f32.shape[1]
    edge = half // LANES
    tile_rows = tile_ref.shape[1]

    @pl.when(step == 0)
    def _():
        for part in range(2):
            for tile in range(tiles):
                if tile < edge:
                    at = slice(tile * LANES, (tile + 1) * LANES)
                    ext_f32[part, tile] = left_ref[part, :, at].astype(jnp.float32)
                elif tile >= tiles - edge:
                    at = slice((tile - tiles + edge) * LANES, (tile - tiles + edge + 1) * LANES)
                    ext_f32[part, tile] = right_ref[part, :, at].astype(jnp.float32)
                else:
                    at = slice((tile - edge) * LANES, (tile - edge + 1) * LANES)
                    ext_f32[part, tile, :half] = above_ref[part, :, at].astype(jnp.float32)
                    ext_f32[part, tile, half : half + tile_rows] = tile_ref[
                        part, :, at
                    ].astype(jnp.float32)
                    ext_f32[part, tile, half + tile_rows :] = below_ref[part, :, at].astype(
                        jnp.float32
                    )
        acc_ref[...] = jnp.zeros(acc_ref.shape, jnp.float32)
        probe_grad_ref[...] = jnp.zeros(probe_grad_ref.shape, jnp.float32)
        power = jnp.zeros((side, side), jnp.float32)
        for mode in range(modes):
            for part in range(2):
                values = probe_ref[mode, part].astype(jnp.float32)
                power += values * values
        scale_ref[0] = 1.0 / (jnp.max(power) + EPSILON)

    row = rows_ref[step]
    col = cols_ref[step]
    tile0 = col // LANES
    lane0 = col % LANES
    width = side // LANES
    lane = lax.broadcasted_iota(jnp.int32, (side, LANES), 1)
    left_part = lane < LANES - lane0
    for part in range(2):
        rolled = [
            pltpu.roll(
                ext_f32[part, tile0 + j, pl.ds(row, side), :], (LANES - lane0) % LANES, 1
            )
            for j in range(width + 1)
        ]
        for j in range(width):
            patch_ref[part, :, j * LANES : (j + 1) * LANES] = jnp.where(
                left_part, rolled[j], rolled[j + 1]
            )

    table_le = table_ref[0]
    table_lo = table_ref[1]
    table_re = table_ref[2]
    table_ro = table_ref[3]
    power_e = jnp.zeros((side, half), jnp.float32)
    power_o = jnp.zeros((side, half), jnp.float32)
    for mode in range(modes):
        wave = []
        for rows in (slice(0, half), slice(half, side)):
            qr = probe_ref[mode, 0, rows, :].astype(jnp.float32)
            qi = probe_ref[mode, 1, rows, :].astype(jnp.float32)
            pr = patch_ref[0, rows, :]
            pi = patch_ref[1, rows, :]
            wave.append((qr * pr - qi * pi, qr * pi + qi * pr))
        (lo_re, lo_im), (hi_re, hi_im) = wave
        sums = jnp.concatenate(
            [(lo_re + hi_re).astype(jnp.bfloat16), (lo_im + hi_im).astype(jnp.bfloat16)], axis=0
        )
        diffs = jnp.concatenate(
            [(lo_re - hi_re).astype(jnp.bfloat16), (lo_im - hi_im).astype(jnp.bfloat16)], axis=0
        )
        evens, odds = [], []
        for half_field in (mm(table_le, sums), mm(table_lo, diffs)):
            re_lo, re_hi = half_field[:half, :half], half_field[:half, half:]
            im_lo, im_hi = half_field[half:, :half], half_field[half:, half:]
            evens.append(
                jnp.concatenate(
                    [(re_lo + re_hi).astype(jnp.bfloat16), (im_lo + im_hi).astype(jnp.bfloat16)],
                    axis=1,
                )
            )
            odds.append(
                jnp.concatenate(
                    [(re_lo - re_hi).astype(jnp.bfloat16), (im_lo - im_hi).astype(jnp.bfloat16)],
                    axis=1,
                )
            )
        far_e = mm(jnp.concatenate(evens, axis=0), table_re)
        far_o = mm(jnp.concatenate(odds, axis=0), table_ro)
        far_ref[mode, 0] = far_e
        far_ref[mode, 1] = far_o
        power_e += far_e[:, :half] * far_e[:, :half] + far_e[:, half:] * far_e[:, half:]
        power_o += far_o[:, :half] * far_o[:, :half] + far_o[:, half:] * far_o[:, half:]

    ratio_e = amp_ref[0, :, :half] * lax.rsqrt(jnp.maximum(power_e, 1.0)) - 1.0
    ratio_o = amp_ref[0, :, half:] * lax.rsqrt(jnp.maximum(power_o, 1.0)) - 1.0

    obj = [[None, None], [None, None]]
    for mode in range(modes):
        far_e = far_ref[mode, 0]
        far_o = far_ref[mode, 1]
        diff_e = jnp.concatenate(
            [
                (far_e[:, :half] * ratio_e).astype(jnp.bfloat16),
                (far_e[:, half:] * ratio_e).astype(jnp.bfloat16),
            ],
            axis=1,
        )
        diff_o = jnp.concatenate(
            [
                (far_o[:, :half] * ratio_o).astype(jnp.bfloat16),
                (far_o[:, half:] * ratio_o).astype(jnp.bfloat16),
            ],
            axis=1,
        )
        u = mm(diff_e, table_le)
        v = mm(diff_o, table_lo)
        total = (u + v).astype(jnp.bfloat16)
        gap = (u - v).astype(jnp.bfloat16)
        backs = []
        for rows in (slice(0, half), slice(half, side)):
            backs.append(
                jnp.concatenate(
                    [
                        jnp.concatenate([total[rows, :half], gap[rows, :half]], axis=1),
                        jnp.concatenate([total[rows, half:], gap[rows, half:]], axis=1),
                    ],
                    axis=0,
                )
            )
        p = mm(table_re, backs[0])
        q = mm(table_ro, backs[1])
        for index, sign in ((0, 1), (1, -1)):
            rows = slice(index * half, (index + 1) * half)
            if sign > 0:
                chi_re = p[:half] + q[:half]
                chi_im = p[half:] + q[half:]
            else:
                chi_re = p[:half] - q[:half]
                chi_im = p[half:] - q[half:]
            qr = probe_ref[mode, 0, rows, :].astype(jnp.float32)
            qi = probe_ref[mode, 1, rows, :].astype(jnp.float32)
            pr = patch_ref[0, rows, :]
            pi = patch_ref[1, rows, :]
            term_re = qr * chi_re + qi * chi_im
            term_im = qr * chi_im - qi * chi_re
            if mode == 0:
                obj[index] = [term_re, term_im]
            else:
                obj[index][0] += term_re
                obj[index][1] += term_im
            probe_grad_ref[mode, 0, rows, :] += pr * chi_re + pi * chi_im
            probe_grad_ref[mode, 1, rows, :] += pr * chi_im - pi * chi_re

    lane_h = lax.broadcasted_iota(jnp.int32, (half, LANES), 1)
    right_part = lane_h >= lane0
    scale = scale_ref[0]
    for index in range(2):
        for part in range(2):
            values = obj[index][part] * scale
            rolled = [
                pltpu.roll(values[:, j * LANES : (j + 1) * LANES], lane0, 1) for j in range(width)
            ]
            where = pl.ds(row + index * half, half)
            for j in range(width + 1):
                above = rolled[j] if j < width else jnp.zeros_like(rolled[0])
                below = rolled[j - 1] if j > 0 else jnp.zeros_like(rolled[0])
                acc_ref[part, tile0 + j, where, :] += jnp.where(right_part, above, below)

    @pl.when(step == pl.num_programs(0) - 1)
    def _():
        for part in range(2):
            for tile in range(tiles):
                values = acc_ref[part, tile]
                if tile < edge:
                    at = slice(tile * LANES, (tile + 1) * LANES)
                    rim_ref[0, part, :, at] = values.astype(rim_ref.dtype)
                elif tile >= tiles - edge:
                    at = slice((tile - tiles + edge) * LANES, (tile - tiles + edge + 1) * LANES)
                    rim_ref[1, part, :, at] = values.astype(rim_ref.dtype)
                else:
                    at = slice((tile - edge) * LANES, (tile - edge + 1) * LANES)
                    grad_ref[part, :, at] = values


def propagate(rows, cols, pieces, probe_low, amplitude, tables):
    count = rows.shape[0]
    modes, _, side, _ = probe_low.shape
    half = side // 2
    tile_rows, tile_cols = pieces[0].shape[1:]
    ext_rows = tile_rows + side
    tiles = (tile_cols + side) // LANES

    def whole(*shape):
        return pl.BlockSpec(
            shape, lambda i, *_: (0,) * len(shape), pipeline_mode=pl.Buffered(1)
        )

    return pl.pallas_call(
        propagate_body,
        out_shape=(
            jax.ShapeDtypeStruct((2, ext_rows, tile_cols), jnp.float32),
            jax.ShapeDtypeStruct((2, 2, ext_rows, half), jnp.bfloat16),
            jax.ShapeDtypeStruct((modes, 2, side, side), jnp.float32),
        ),
        grid_spec=pltpu.PrefetchScalarGridSpec(
            num_scalar_prefetch=2,
            grid=(count,),
            in_specs=[whole(*piece.shape) for piece in pieces]
            + [
                whole(*probe_low.shape),
                pl.BlockSpec((1, side, side), lambda i, *_: (i, 0, 0)),
                whole(*tables.shape),
            ],
            out_specs=(
                whole(2, ext_rows, tile_cols),
                whole(2, 2, ext_rows, half),
                whole(modes, 2, side, side),
            ),
            scratch_shapes=[
                pltpu.VMEM((2, tiles, ext_rows, LANES), jnp.float32),
                pltpu.VMEM((2, side, side), jnp.float32),
                pltpu.VMEM((modes, 2, side, side), jnp.float32),
                pltpu.VMEM((2, tiles, ext_rows, LANES), jnp.float32),
                pltpu.SMEM((1,), jnp.float32),
            ],
        ),
        name="propagate",
    )(rows, cols, *pieces, probe_low, amplitude, tables)


def exchange_steps():
    steps = []
    bit = 1
    while bit < lax.axis_size("obj"):
        steps.append(("obj", bit, jnp.bfloat16))
        bit *= 2
    bit = 2
    while bit < lax.axis_size("dp"):
        steps.append(("dp", bit, jnp.bfloat16))
        bit *= 2
    if lax.axis_size("dp") > 1:
        steps.append(("dp", 1, jnp.float32))
    return steps


def halve(values, axis, bit):
    rows = values.shape[0] // 2
    upper = (lax.axis_index(axis) // bit) % 2
    keep = lax.dynamic_slice_in_dim(values, upper * rows, rows, 0)
    send = lax.dynamic_slice_in_dim(values, (1 - upper) * rows, rows, 0)
    return keep, send


def sum_to_share(values):
    for axis, bit, kind in exchange_steps():
        keep, send = halve(values, axis, bit)
        got = swap_bit(send.astype(kind), axis, bit)
        values = keep + got.astype(values.dtype)
    return values


def own_share(values):
    for axis, bit, _ in exchange_steps():
        values = halve(values, axis, bit)[0]
    return values


def join_shares(values):
    steps = exchange_steps()
    for index in range(len(steps) - 1, -1, -1):
        axis, bit, _ = steps[index]
        got = swap_bit(values, axis, bit)
        lower = (lax.axis_index(axis) // bit) % 2 == 0
        values = jnp.concatenate(
            [jnp.where(lower, values, got), jnp.where(lower, got, values)], axis=0
        )
    return values


def fold_rims(grad, rims, half, tile_rows, tile_cols):
    left, right = rims[0], rims[1]
    from_left, from_right = neighbours(left, right, "obj")
    wide = jnp.zeros((2, grad.shape[1], tile_cols - 2 * half), from_left.dtype)
    total = grad + jnp.concatenate([from_left, wide, from_right], axis=2).astype(jnp.float32)
    low = total.astype(jnp.bfloat16)
    from_above, from_below = neighbours(low[:, :half], low[:, -half:], "dp")
    tall = jnp.zeros((2, tile_rows - 2 * half, tile_cols), from_above.dtype)
    inner = total[:, half : half + tile_rows]
    return inner + jnp.concatenate([from_above, tall, from_below], axis=1).astype(jnp.float32)


def gather_rims(tile, half):
    above, below = neighbours(tile[:, :half], tile[:, -half:], "dp")
    first = jnp.concatenate([above[:, :, :half], tile[:, :, :half], below[:, :, :half]], axis=1)
    last = jnp.concatenate([above[:, :, -half:], tile[:, :, -half:], below[:, :, -half:]], axis=1)
    left, right = neighbours(first, last, "obj")
    return tile, above, below, left, right


def shards(object_field, probe_modes, amplitude, offsets):
    side = probe_modes.shape[2]
    half = side // 2
    tile_rows = object_field.shape[1]
    tile_cols = object_field.shape[2]
    count = offsets.shape[0]
    devices = lax.axis_size("dp") * lax.axis_size("obj")
    total_positions = count * devices
    tables = split_tables(side)
    amplitude = even_odd(amplitude)
    top_rows = offsets[:, 0] - lax.axis_index("dp") * tile_rows + half
    left_cols = offsets[:, 1] - lax.axis_index("obj") * tile_cols + half
    current = object_field
    probe_low = probe_modes.astype(jnp.bfloat16)
    probe_share = own_share(probe_modes.reshape(-1, side))
    pieces = gather_rims(current.astype(jnp.bfloat16), half)
    for turn in range(ITERS):
        grad, rims, probe_terms = propagate(
            top_rows, left_cols, pieces, probe_low, amplitude, tables
        )
        current = current + fold_rims(grad, rims, half, tile_rows, tile_cols)
        summed = sum_to_share(probe_terms.reshape(-1, side))
        probe_share = probe_share + summed / total_positions
        if turn + 1 < ITERS:
            pieces = gather_rims(current.astype(jnp.bfloat16), half)
            probe_low = join_shares(probe_share.astype(jnp.bfloat16)).reshape(
                probe_modes.shape
            )
        else:
            probe = join_shares(probe_share).reshape(probe_modes.shape)
    return (current, probe)


def solution(mesh):
    in_specs = (P(None, "dp", "obj"), P(), P(("dp", "obj"), None, None), P(("dp", "obj"), None))
    out_specs = (P(None, "dp", "obj"), P())
    return jax.shard_map(shards, mesh=mesh, in_specs=in_specs, out_specs=out_specs, check_vma=False)
```

```python
import jax
import jax.numpy as jnp
import numpy as np
from jax import lax
from jax.experimental import pallas as pl
from jax.experimental.pallas import tpu as pltpu
from jax.sharding import PartitionSpec as P


ITERS = 2


EPSILON = 1e-06


LANES = 128


def swap_bit(values, axis, bit):
    return lax.ppermute(values, axis, [(i, i ^ bit) for i in range(lax.axis_size(axis))])


def shift_both(before, after, axis):
    up = [(i, i + 1) for i in range(lax.axis_size(axis) - 1)]
    previous = lax.ppermute(after, axis, up)
    following = lax.ppermute(before, axis, [(target, source) for source, target in up])
    return previous, following


def swap_both(outer, inner, axis):
    count = lax.axis_size(axis)
    inner_pairs = [(i, i ^ 1) for i in range(count)]
    outer_pairs = [(i, i + 1) for i in range(1, count - 1, 2)]
    outer_pairs = outer_pairs + [(target, source) for source, target in outer_pairs]
    outer = lax.ppermute(outer, axis, outer_pairs)
    inner = lax.ppermute(inner, axis, inner_pairs)
    return outer, inner


def pick(condition, first, second):
    return jnp.where(condition, first, second), jnp.where(condition, second, first)


def dft_tables(length):
    counter = np.arange(length, dtype=np.int32)
    phase_steps = counter[:, None] * counter[None, :] % length
    angle_grid = phase_steps.astype(np.float32) * np.float32(2.0 * np.pi / length)
    norm_factor = np.float32(1.0) / np.sqrt(np.float32(length))
    return (np.cos(angle_grid) * norm_factor, -np.sin(angle_grid) * norm_factor)


def split_tables(length):
    real_table, imag_table = dft_tables(length)
    half = length // 2
    lefts = []
    for first in (0, 1):
        re = real_table[first::2, :half]
        im = imag_table[first::2, :half]
        lefts.append(np.block([[re, -im], [im, re]]))
    return jnp.asarray(np.stack(lefts + [lefts[0].T, lefts[1].T]), jnp.bfloat16)


def even_odd(values):
    side = values.shape[-1]
    order = np.concatenate([np.arange(0, side, 2), np.arange(1, side, 2)])
    pick = jnp.asarray(np.arange(side)[:, None] == order[None, :], jnp.float32)
    right = jnp.einsum(
        "brc,ck->brk", values, pick, precision=lax.Precision.HIGHEST,
        preferred_element_type=jnp.float32,
    )
    return jnp.einsum(
        "rk,brc->bkc", pick, right, precision=lax.Precision.HIGHEST,
        preferred_element_type=jnp.float32,
    )


def mm(left, right):
    return jnp.dot(left, right, preferred_element_type=jnp.float32)


def propagate_body(
    rows_ref, cols_ref, flag_ref, tile_ref, above_ref, below_ref, outer_ref, inner_ref, own_ref,
    other_ref, amp_ref, table_ref, grad_ref, rim_outer_ref, rim_inner_ref, keep_ref, send_ref,
    ext_f32, patch_ref, far_ref, acc_ref, probe_ref, probe_acc, scale_ref,
):
    modes, _, side, _ = probe_ref.shape
    half = side // 2
    step = pl.program_id(0)
    tiles = ext_f32.shape[1]
    edge = half // LANES
    tile_rows = tile_ref.shape[1]
    odd = flag_ref[0]
    upper = flag_ref[1]
    share = modes // 2

    @pl.when(step == 0)
    def _():
        probe_ref[pl.ds(upper * share, share)] = own_ref[...].astype(jnp.float32)
        probe_ref[pl.ds((1 - upper) * share, share)] = other_ref[...].astype(jnp.float32)
        for part in range(2):
            for tile in range(edge):
                at = slice(tile * LANES, (tile + 1) * LANES)
                last = (tiles - edge) * odd + tile
                first = (tiles - edge) * (1 - odd) + tile
                ext_f32[part, last] = outer_ref[part, :, at].astype(jnp.float32)
                ext_f32[part, first] = inner_ref[part, :, at].astype(jnp.float32)
            for tile in range(edge, tiles - edge):
                at = slice((tile - edge) * LANES, (tile - edge + 1) * LANES)
                ext_f32[part, tile, :half] = above_ref[part, :, at].astype(jnp.float32)
                ext_f32[part, tile, half : half + tile_rows] = tile_ref[part, :, at].astype(
                    jnp.float32
                )
                ext_f32[part, tile, half + tile_rows :] = below_ref[part, :, at].astype(
                    jnp.float32
                )
        acc_ref[...] = jnp.zeros(acc_ref.shape, jnp.float32)
        probe_acc[...] = jnp.zeros(probe_acc.shape, jnp.float32)
        power = jnp.zeros((side, side), jnp.float32)
        for mode in range(modes):
            for part in range(2):
                values = probe_ref[mode, part]
                power += values * values
        scale_ref[0] = 1.0 / (jnp.max(power) + EPSILON)

    row = rows_ref[step]
    col = cols_ref[step]
    tile0 = col // LANES
    lane0 = col % LANES
    width = side // LANES
    lane = lax.broadcasted_iota(jnp.int32, (side, LANES), 1)
    left_part = lane < LANES - lane0
    for part in range(2):
        rolled = [
            pltpu.roll(
                ext_f32[part, tile0 + j, pl.ds(row, side), :], (LANES - lane0) % LANES, 1
            )
            for j in range(width + 1)
        ]
        for j in range(width):
            patch_ref[part, :, j * LANES : (j + 1) * LANES] = jnp.where(
                left_part, rolled[j], rolled[j + 1]
            )

    table_le = table_ref[0]
    table_lo = table_ref[1]
    table_re = table_ref[2]
    table_ro = table_ref[3]
    power_e = jnp.zeros((side, half), jnp.float32)
    power_o = jnp.zeros((side, half), jnp.float32)
    for mode in range(modes):
        wave = []
        for rows in (slice(0, half), slice(half, side)):
            qr = probe_ref[mode, 0, rows, :]
            qi = probe_ref[mode, 1, rows, :]
            pr = patch_ref[0, rows, :]
            pi = patch_ref[1, rows, :]
            wave.append((qr * pr - qi * pi, qr * pi + qi * pr))
        (lo_re, lo_im), (hi_re, hi_im) = wave
        sums = jnp.concatenate(
            [(lo_re + hi_re).astype(jnp.bfloat16), (lo_im + hi_im).astype(jnp.bfloat16)], axis=0
        )
        diffs = jnp.concatenate(
            [(lo_re - hi_re).astype(jnp.bfloat16), (lo_im - hi_im).astype(jnp.bfloat16)], axis=0
        )
        evens, odds = [], []
        for half_field in (mm(table_le, sums), mm(table_lo, diffs)):
            re_lo, re_hi = half_field[:half, :half], half_field[:half, half:]
            im_lo, im_hi = half_field[half:, :half], half_field[half:, half:]
            evens.append(
                jnp.concatenate(
                    [(re_lo + re_hi).astype(jnp.bfloat16), (im_lo + im_hi).astype(jnp.bfloat16)],
                    axis=1,
                )
            )
            odds.append(
                jnp.concatenate(
                    [(re_lo - re_hi).astype(jnp.bfloat16), (im_lo - im_hi).astype(jnp.bfloat16)],
                    axis=1,
                )
            )
        far_e = mm(jnp.concatenate(evens, axis=0), table_re)
        far_o = mm(jnp.concatenate(odds, axis=0), table_ro)
        far_ref[mode, 0] = far_e
        far_ref[mode, 1] = far_o
        power_e += far_e[:, :half] * far_e[:, :half] + far_e[:, half:] * far_e[:, half:]
        power_o += far_o[:, :half] * far_o[:, :half] + far_o[:, half:] * far_o[:, half:]

    ratio_e = amp_ref[0, :, :half] * lax.rsqrt(jnp.maximum(power_e, 1.0)) - 1.0
    ratio_o = amp_ref[0, :, half:] * lax.rsqrt(jnp.maximum(power_o, 1.0)) - 1.0

    obj = [[None, None], [None, None]]
    for mode in range(modes):
        far_e = far_ref[mode, 0]
        far_o = far_ref[mode, 1]
        diff_e = jnp.concatenate(
            [
                (far_e[:, :half] * ratio_e).astype(jnp.bfloat16),
                (far_e[:, half:] * ratio_e).astype(jnp.bfloat16),
            ],
            axis=1,
        )
        diff_o = jnp.concatenate(
            [
                (far_o[:, :half] * ratio_o).astype(jnp.bfloat16),
                (far_o[:, half:] * ratio_o).astype(jnp.bfloat16),
            ],
            axis=1,
        )
        u = mm(diff_e, table_le)
        v = mm(diff_o, table_lo)
        total = (u + v).astype(jnp.bfloat16)
        gap = (u - v).astype(jnp.bfloat16)
        backs = []
        for rows in (slice(0, half), slice(half, side)):
            backs.append(
                jnp.concatenate(
                    [
                        jnp.concatenate([total[rows, :half], gap[rows, :half]], axis=1),
                        jnp.concatenate([total[rows, half:], gap[rows, half:]], axis=1),
                    ],
                    axis=0,
                )
            )
        p = mm(table_re, backs[0])
        q = mm(table_ro, backs[1])
        for index, sign in ((0, 1), (1, -1)):
            rows = slice(index * half, (index + 1) * half)
            if sign > 0:
                chi_re = p[:half] + q[:half]
                chi_im = p[half:] + q[half:]
            else:
                chi_re = p[:half] - q[:half]
                chi_im = p[half:] - q[half:]
            qr = probe_ref[mode, 0, rows, :]
            qi = probe_ref[mode, 1, rows, :]
            pr = patch_ref[0, rows, :]
            pi = patch_ref[1, rows, :]
            term_re = qr * chi_re + qi * chi_im
            term_im = qr * chi_im - qi * chi_re
            if mode == 0:
                obj[index] = [term_re, term_im]
            else:
                obj[index][0] += term_re
                obj[index][1] += term_im
            probe_acc[mode, 0, rows, :] += pr * chi_re + pi * chi_im
            probe_acc[mode, 1, rows, :] += pr * chi_im - pi * chi_re

    lane_h = lax.broadcasted_iota(jnp.int32, (half, LANES), 1)
    right_part = lane_h >= lane0
    scale = scale_ref[0]
    for index in range(2):
        for part in range(2):
            values = obj[index][part] * scale
            rolled = [
                pltpu.roll(values[:, j * LANES : (j + 1) * LANES], lane0, 1) for j in range(width)
            ]
            where = pl.ds(row + index * half, half)
            for j in range(width + 1):
                above = rolled[j] if j < width else jnp.zeros_like(rolled[0])
                below = rolled[j - 1] if j > 0 else jnp.zeros_like(rolled[0])
                acc_ref[part, tile0 + j, where, :] += jnp.where(right_part, above, below)

    @pl.when(step == pl.num_programs(0) - 1)
    def _():
        keep_ref[...] = probe_acc[pl.ds(upper * share, share)]
        send_ref[...] = probe_acc[pl.ds((1 - upper) * share, share)].astype(send_ref.dtype)
        for part in range(2):
            for tile in range(edge):
                at = slice(tile * LANES, (tile + 1) * LANES)
                last = (tiles - edge) * odd + tile
                first = (tiles - edge) * (1 - odd) + tile
                rim_outer_ref[part, :, at] = acc_ref[part, last].astype(rim_outer_ref.dtype)
                rim_inner_ref[part, :, at] = acc_ref[part, first].astype(rim_inner_ref.dtype)
            for tile in range(edge, tiles - edge):
                at = slice((tile - edge) * LANES, (tile - edge + 1) * LANES)
                grad_ref[part, :, at] = acc_ref[part, tile]


def propagate(rows, cols, flags, pieces, probe_parts, amplitude, tables):
    count = rows.shape[0]
    share, _, side, _ = probe_parts[0].shape
    modes = 2 * share
    half = side // 2
    tile_rows, tile_cols = pieces[0].shape[1:]
    ext_rows = tile_rows + side
    tiles = (tile_cols + side) // LANES

    def whole(*shape):
        return pl.BlockSpec(
            shape, lambda i, *_: (0,) * len(shape), pipeline_mode=pl.Buffered(1)
        )

    outs = (
        jax.ShapeDtypeStruct((2, ext_rows, tile_cols), jnp.float32),
        jax.ShapeDtypeStruct((2, ext_rows, half), jnp.bfloat16),
        jax.ShapeDtypeStruct((2, ext_rows, half), jnp.bfloat16),
        jax.ShapeDtypeStruct((share, 2, side, side), jnp.float32),
        jax.ShapeDtypeStruct((share, 2, side, side), jnp.bfloat16),
    )
    return pl.pallas_call(
        propagate_body,
        out_shape=outs,
        grid_spec=pltpu.PrefetchScalarGridSpec(
            num_scalar_prefetch=3,
            grid=(count,),
            in_specs=[whole(*piece.shape) for piece in pieces]
            + [whole(*part.shape) for part in probe_parts]
            + [
                pl.BlockSpec((1, side, side), lambda i, *_: (i, 0, 0)),
                whole(*tables.shape),
            ],
            out_specs=tuple(whole(*out.shape) for out in outs),
            scratch_shapes=[
                pltpu.VMEM((2, tiles, ext_rows, LANES), jnp.float32),
                pltpu.VMEM((2, side, side), jnp.float32),
                pltpu.VMEM((modes, 2, side, side), jnp.float32),
                pltpu.VMEM((2, tiles, ext_rows, LANES), jnp.float32),
                pltpu.VMEM((modes, 2, side, side), jnp.float32),
                pltpu.VMEM((modes, 2, side, side), jnp.float32),
                pltpu.SMEM((1,), jnp.float32),
            ],
        ),
        name="propagate",
    )(rows, cols, flags, *pieces, *probe_parts, amplitude, tables)


def exchange_steps():
    steps = []
    bit = 1
    while bit < lax.axis_size("obj"):
        steps.append(("obj", bit))
        bit *= 2
    bit = 2
    while bit < lax.axis_size("dp"):
        steps.append(("dp", bit))
        bit *= 2
    return steps


def upper_of(axis, bit):
    return (lax.axis_index(axis) // bit) % 2


def halve(values, axis, bit):
    rows = values.shape[0] // 2
    upper = upper_of(axis, bit)
    keep = lax.dynamic_slice_in_dim(values, upper * rows, rows, 0)
    send = lax.dynamic_slice_in_dim(values, (1 - upper) * rows, rows, 0)
    return keep, send


def sum_to_share(keep, send):
    for index, (axis, bit) in enumerate(exchange_steps()):
        if index > 0:
            keep, send = halve(values, axis, bit)
        got = swap_bit(send.astype(jnp.bfloat16), axis, bit)
        values = keep + got.astype(keep.dtype)
    got = swap_bit(values, "dp", 1)
    return values + got


def own_share(values):
    for axis, bit in exchange_steps():
        values = halve(values, axis, bit)[0]
    return values


def join_shares(values):
    steps = exchange_steps()
    for index in range(len(steps) - 1, -1, -1):
        axis, bit = steps[index]
        got = swap_bit(values, axis, bit)
        if index == 0:
            return values, got
        values = jnp.concatenate(pick(upper_of(axis, bit) == 0, values, got), axis=0)


def fold_rims(current, grad, rim_outer, rim_inner, half):
    tile_rows, tile_cols = current.shape[1:]
    odd = lax.axis_index("obj") % 2 == 1
    outer, inner = swap_both(rim_outer, rim_inner, "obj")
    left, right = pick(odd, inner, outer)
    wide = jnp.zeros((2, grad.shape[1], tile_cols - 2 * half), left.dtype)
    total = grad + jnp.concatenate([left, wide, right], axis=2).astype(jnp.float32)
    low = total.astype(jnp.bfloat16)
    first, last = low[:, :half], low[:, -half:]
    above, below = shift_both(first, last, "dp")
    tall = jnp.zeros((2, tile_rows - 2 * half, tile_cols), above.dtype)
    rows = jnp.concatenate([above, tall, below], axis=1).astype(jnp.float32)
    current = current + (total[:, half : half + tile_rows] + rows)
    return current, current.astype(jnp.bfloat16)


def gather_rims(tile, half):
    low = lambda values: values.astype(jnp.bfloat16)
    above, below = shift_both(low(tile[:, :half]), low(tile[:, -half:]), "dp")
    tile = low(tile)
    first = jnp.concatenate([above[:, :, :half], tile[:, :, :half], below[:, :, :half]], axis=1)
    last = jnp.concatenate([above[:, :, -half:], tile[:, :, -half:], below[:, :, -half:]], axis=1)
    odd = lax.axis_index("obj") % 2 == 1
    outer, inner = swap_both(*pick(odd, last, first), "obj")
    return tile, above, below, outer, inner


def shards(object_field, probe_modes, amplitude, offsets):
    modes, _, side, _ = probe_modes.shape
    half = side // 2
    tile_rows = object_field.shape[1]
    tile_cols = object_field.shape[2]
    count = offsets.shape[0]
    devices = lax.axis_size("dp") * lax.axis_size("obj")
    total_positions = count * devices
    tables = split_tables(side)
    amplitude = even_odd(amplitude)
    top_rows = offsets[:, 0] - lax.axis_index("dp") * tile_rows + half
    left_cols = offsets[:, 1] - lax.axis_index("obj") * tile_cols + half
    upper = upper_of("obj", 1)
    flags = jnp.stack([lax.axis_index("obj") % 2, upper])
    split = (modes // 2, 2, side, side)
    current = object_field
    probe_parts = [
        half_modes.astype(jnp.bfloat16).reshape(split)
        for half_modes in halve(probe_modes.reshape(-1, side), "obj", 1)
    ]
    probe_share = own_share(probe_modes.reshape(-1, side))
    pieces = gather_rims(current, half)
    for turn in range(ITERS):
        grad, rim_outer, rim_inner, keep, send = propagate(
            top_rows, left_cols, flags, pieces, probe_parts, amplitude, tables
        )
        current, low_tile = fold_rims(current, grad, rim_outer, rim_inner, half)
        summed = sum_to_share(keep.reshape(-1, side), send.reshape(-1, side))
        probe_share = probe_share + summed / total_positions
        if turn + 1 < ITERS:
            pieces = gather_rims(low_tile, half)
            low_share = probe_share.astype(jnp.bfloat16)
            parts = join_shares(low_share)
            probe_parts = [part.reshape(split) for part in parts]
        else:
            rest = (probe_share - low_share.astype(jnp.float32)).astype(jnp.bfloat16)
            parts = [
                part.astype(jnp.float32) + more.astype(jnp.float32)
                for part, more in zip(parts, join_shares(rest))
            ]
            parts = pick(upper == 0, *parts)
            probe = jnp.concatenate(parts, axis=0).reshape(probe_modes.shape)
    return (current, probe)


def solution(mesh):
    in_specs = (P(None, "dp", "obj"), P(), P(("dp", "obj"), None, None), P(("dp", "obj"), None))
    out_specs = (P(None, "dp", "obj"), P())
    return jax.shard_map(shards, mesh=mesh, in_specs=in_specs, out_specs=out_specs, check_vma=False)
```

```python
import jax
import jax.numpy as jnp
import numpy as np
from jax import lax
from jax.experimental import pallas as pl
from jax.experimental.pallas import tpu as pltpu
from jax.sharding import PartitionSpec as P


ITERS = 2


EPSILON = 1e-06


LANES = 128


def swap_bit(values, axis, bit):
    return lax.ppermute(values, axis, [(i, i ^ bit) for i in range(lax.axis_size(axis))])


def shift_both(before, after, axis):
    up = [(i, i + 1) for i in range(lax.axis_size(axis) - 1)]
    previous = lax.ppermute(after, axis, up)
    following = lax.ppermute(before, axis, [(target, source) for source, target in up])
    return previous, following


def swap_both(outer, inner, axis):
    count = lax.axis_size(axis)
    inner_pairs = [(i, i ^ 1) for i in range(count)]
    outer_pairs = [(i, i + 1) for i in range(1, count - 1, 2)]
    outer_pairs = outer_pairs + [(target, source) for source, target in outer_pairs]
    outer = lax.ppermute(outer, axis, outer_pairs)
    inner = lax.ppermute(inner, axis, inner_pairs)
    return outer, inner


def pick(condition, first, second):
    return jnp.where(condition, first, second), jnp.where(condition, second, first)


def dft_tables(length):
    counter = np.arange(length, dtype=np.int32)
    phase_steps = counter[:, None] * counter[None, :] % length
    angle_grid = phase_steps.astype(np.float32) * np.float32(2.0 * np.pi / length)
    norm_factor = np.float32(1.0) / np.sqrt(np.float32(length))
    return (np.cos(angle_grid) * norm_factor, -np.sin(angle_grid) * norm_factor)


def split_tables(length):
    real_table, imag_table = dft_tables(length)
    half = length // 2
    lefts = []
    for first in (0, 1):
        re = real_table[first::2, :half]
        im = imag_table[first::2, :half]
        lefts.append(np.block([[re, -im], [im, re]]))
    return jnp.asarray(np.stack(lefts + [lefts[0].T, lefts[1].T]), jnp.bfloat16)


def even_odd(values):
    side = values.shape[-1]
    order = np.concatenate([np.arange(0, side, 2), np.arange(1, side, 2)])
    pick = jnp.asarray(np.arange(side)[:, None] == order[None, :], jnp.float32)
    right = jnp.einsum(
        "brc,ck->brk", values, pick, precision=lax.Precision.HIGHEST,
        preferred_element_type=jnp.float32,
    )
    return jnp.einsum(
        "rk,brc->bkc", pick, right, precision=lax.Precision.HIGHEST,
        preferred_element_type=jnp.float32,
    )


def mm(left, right):
    return jnp.dot(left, right, preferred_element_type=jnp.float32)


def propagate_body(
    rows_ref, cols_ref, flag_ref, tile_ref, above_ref, below_ref, outer_ref, inner_ref, own_ref,
    other_ref, amp_ref, table_ref, grad_ref, rim_outer_ref, rim_inner_ref, keep_ref, send_ref,
    ext_f32, patch_ref, far_ref, acc_ref, probe_ref, probe_acc, scale_ref,
):
    modes, _, side, _ = probe_ref.shape
    half = side // 2
    step = pl.program_id(0)
    tiles = ext_f32.shape[1]
    edge = half // LANES
    tile_rows = tile_ref.shape[1]
    odd = flag_ref[0]
    upper = flag_ref[1]
    share = modes // 2

    @pl.when(step == 0)
    def _():
        probe_ref[pl.ds(upper * share, share)] = own_ref[...].astype(jnp.float32)
        probe_ref[pl.ds((1 - upper) * share, share)] = other_ref[...].astype(jnp.float32)
        for part in range(2):
            for tile in range(edge):
                at = slice(tile * LANES, (tile + 1) * LANES)
                last = (tiles - edge) * odd + tile
                first = (tiles - edge) * (1 - odd) + tile
                ext_f32[part, last] = outer_ref[part, :, at].astype(jnp.float32)
                ext_f32[part, first] = inner_ref[part, :, at].astype(jnp.float32)
            for tile in range(edge, tiles - edge):
                at = slice((tile - edge) * LANES, (tile - edge + 1) * LANES)
                ext_f32[part, tile, :half] = above_ref[part, :, at].astype(jnp.float32)
                ext_f32[part, tile, half : half + tile_rows] = tile_ref[part, :, at].astype(
                    jnp.float32
                )
                ext_f32[part, tile, half + tile_rows :] = below_ref[part, :, at].astype(
                    jnp.float32
                )
        acc_ref[...] = jnp.zeros(acc_ref.shape, jnp.float32)
        probe_acc[...] = jnp.zeros(probe_acc.shape, jnp.float32)
        power = jnp.zeros((side, side), jnp.float32)
        for mode in range(modes):
            for part in range(2):
                values = probe_ref[mode, part]
                power += values * values
        scale_ref[0] = 1.0 / (jnp.max(power) + EPSILON)

    row = rows_ref[step]
    col = cols_ref[step]
    tile0 = col // LANES
    lane0 = col % LANES
    width = side // LANES
    lane = lax.broadcasted_iota(jnp.int32, (side, LANES), 1)
    left_part = lane < LANES - lane0
    for part in range(2):
        rolled = [
            pltpu.roll(
                ext_f32[part, tile0 + j, pl.ds(row, side), :], (LANES - lane0) % LANES, 1
            )
            for j in range(width + 1)
        ]
        for j in range(width):
            patch_ref[part, :, j * LANES : (j + 1) * LANES] = jnp.where(
                left_part, rolled[j], rolled[j + 1]
            )

    table_le = table_ref[0]
    table_lo = table_ref[1]
    table_re = table_ref[2]
    table_ro = table_ref[3]
    power_e = jnp.zeros((side, half), jnp.float32)
    power_o = jnp.zeros((side, half), jnp.float32)
    for mode in range(modes):
        wave = []
        for rows in (slice(0, half), slice(half, side)):
            qr = probe_ref[mode, 0, rows, :]
            qi = probe_ref[mode, 1, rows, :]
            pr = patch_ref[0, rows, :]
            pi = patch_ref[1, rows, :]
            wave.append((qr * pr - qi * pi, qr * pi + qi * pr))
        (lo_re, lo_im), (hi_re, hi_im) = wave
        sums = jnp.concatenate(
            [(lo_re + hi_re).astype(jnp.bfloat16), (lo_im + hi_im).astype(jnp.bfloat16)], axis=0
        )
        diffs = jnp.concatenate(
            [(lo_re - hi_re).astype(jnp.bfloat16), (lo_im - hi_im).astype(jnp.bfloat16)], axis=0
        )
        evens, odds = [], []
        for half_field in (mm(table_le, sums), mm(table_lo, diffs)):
            re_lo, re_hi = half_field[:half, :half], half_field[:half, half:]
            im_lo, im_hi = half_field[half:, :half], half_field[half:, half:]
            evens.append(
                jnp.concatenate(
                    [(re_lo + re_hi).astype(jnp.bfloat16), (im_lo + im_hi).astype(jnp.bfloat16)],
                    axis=1,
                )
            )
            odds.append(
                jnp.concatenate(
                    [(re_lo - re_hi).astype(jnp.bfloat16), (im_lo - im_hi).astype(jnp.bfloat16)],
                    axis=1,
                )
            )
        far_e = mm(jnp.concatenate(evens, axis=0), table_re)
        far_o = mm(jnp.concatenate(odds, axis=0), table_ro)
        far_ref[mode, 0] = far_e
        far_ref[mode, 1] = far_o
        power_e += far_e[:, :half] * far_e[:, :half] + far_e[:, half:] * far_e[:, half:]
        power_o += far_o[:, :half] * far_o[:, :half] + far_o[:, half:] * far_o[:, half:]

    ratio_e = amp_ref[0, :, :half] * lax.rsqrt(jnp.maximum(power_e, 1.0)) - 1.0
    ratio_o = amp_ref[0, :, half:] * lax.rsqrt(jnp.maximum(power_o, 1.0)) - 1.0

    obj = [[None, None], [None, None]]
    for mode in range(modes):
        far_e = far_ref[mode, 0]
        far_o = far_ref[mode, 1]
        diff_e = jnp.concatenate(
            [
                (far_e[:, :half] * ratio_e).astype(jnp.bfloat16),
                (far_e[:, half:] * ratio_e).astype(jnp.bfloat16),
            ],
            axis=1,
        )
        diff_o = jnp.concatenate(
            [
                (far_o[:, :half] * ratio_o).astype(jnp.bfloat16),
                (far_o[:, half:] * ratio_o).astype(jnp.bfloat16),
            ],
            axis=1,
        )
        u = mm(diff_e, table_le)
        v = mm(diff_o, table_lo)
        total = (u + v).astype(jnp.bfloat16)
        gap = (u - v).astype(jnp.bfloat16)
        backs = []
        for rows in (slice(0, half), slice(half, side)):
            backs.append(
                jnp.concatenate(
                    [
                        jnp.concatenate([total[rows, :half], gap[rows, :half]], axis=1),
                        jnp.concatenate([total[rows, half:], gap[rows, half:]], axis=1),
                    ],
                    axis=0,
                )
            )
        p = mm(table_re, backs[0])
        q = mm(table_ro, backs[1])
        for index, sign in ((0, 1), (1, -1)):
            rows = slice(index * half, (index + 1) * half)
            if sign > 0:
                chi_re = p[:half] + q[:half]
                chi_im = p[half:] + q[half:]
            else:
                chi_re = p[:half] - q[:half]
                chi_im = p[half:] - q[half:]
            qr = probe_ref[mode, 0, rows, :]
            qi = probe_ref[mode, 1, rows, :]
            pr = patch_ref[0, rows, :]
            pi = patch_ref[1, rows, :]
            term_re = qr * chi_re + qi * chi_im
            term_im = qr * chi_im - qi * chi_re
            if mode == 0:
                obj[index] = [term_re, term_im]
            else:
                obj[index][0] += term_re
                obj[index][1] += term_im
            probe_acc[mode, 0, rows, :] += pr * chi_re + pi * chi_im
            probe_acc[mode, 1, rows, :] += pr * chi_im - pi * chi_re

    lane_h = lax.broadcasted_iota(jnp.int32, (half, LANES), 1)
    right_part = lane_h >= lane0
    scale = scale_ref[0]
    for index in range(2):
        for part in range(2):
            values = obj[index][part] * scale
            rolled = [
                pltpu.roll(values[:, j * LANES : (j + 1) * LANES], lane0, 1) for j in range(width)
            ]
            where = pl.ds(row + index * half, half)
            for j in range(width + 1):
                above = rolled[j] if j < width else jnp.zeros_like(rolled[0])
                below = rolled[j - 1] if j > 0 else jnp.zeros_like(rolled[0])
                acc_ref[part, tile0 + j, where, :] += jnp.where(right_part, above, below)

    @pl.when(step == pl.num_programs(0) - 1)
    def _():
        keep_ref[...] = probe_acc[pl.ds(upper * share, share)]
        send_ref[...] = probe_acc[pl.ds((1 - upper) * share, share)].astype(send_ref.dtype)
        for part in range(2):
            for tile in range(edge):
                at = slice(tile * LANES, (tile + 1) * LANES)
                last = (tiles - edge) * odd + tile
                first = (tiles - edge) * (1 - odd) + tile
                rim_outer_ref[part, :, at] = acc_ref[part, last].astype(rim_outer_ref.dtype)
                rim_inner_ref[part, :, at] = acc_ref[part, first].astype(rim_inner_ref.dtype)
            for tile in range(edge, tiles - edge):
                at = slice((tile - edge) * LANES, (tile - edge + 1) * LANES)
                grad_ref[part, :, at] = acc_ref[part, tile]


def propagate(rows, cols, flags, pieces, probe_parts, amplitude, tables):
    count = rows.shape[0]
    share, _, side, _ = probe_parts[0].shape
    modes = 2 * share
    half = side // 2
    tile_rows, tile_cols = pieces[0].shape[1:]
    ext_rows = tile_rows + side
    tiles = (tile_cols + side) // LANES

    def whole(*shape):
        return pl.BlockSpec(
            shape, lambda i, *_: (0,) * len(shape), pipeline_mode=pl.Buffered(1)
        )

    outs = (
        jax.ShapeDtypeStruct((2, ext_rows, tile_cols), jnp.float32),
        jax.ShapeDtypeStruct((2, ext_rows, half), jnp.bfloat16),
        jax.ShapeDtypeStruct((2, ext_rows, half), jnp.bfloat16),
        jax.ShapeDtypeStruct((share, 2, side, side), jnp.float32),
        jax.ShapeDtypeStruct((share, 2, side, side), jnp.bfloat16),
    )
    return pl.pallas_call(
        propagate_body,
        out_shape=outs,
        grid_spec=pltpu.PrefetchScalarGridSpec(
            num_scalar_prefetch=3,
            grid=(count,),
            in_specs=[whole(*piece.shape) for piece in pieces]
            + [whole(*part.shape) for part in probe_parts]
            + [
                pl.BlockSpec((1, side, side), lambda i, *_: (i, 0, 0)),
                whole(*tables.shape),
            ],
            out_specs=tuple(whole(*out.shape) for out in outs),
            scratch_shapes=[
                pltpu.VMEM((2, tiles, ext_rows, LANES), jnp.float32),
                pltpu.VMEM((2, side, side), jnp.float32),
                pltpu.VMEM((modes, 2, side, side), jnp.float32),
                pltpu.VMEM((2, tiles, ext_rows, LANES), jnp.float32),
                pltpu.VMEM((modes, 2, side, side), jnp.float32),
                pltpu.VMEM((modes, 2, side, side), jnp.float32),
                pltpu.SMEM((1,), jnp.float32),
            ],
        ),
        name="propagate",
    )(rows, cols, flags, *pieces, *probe_parts, amplitude, tables)


def exchange_steps():
    steps = []
    bit = 1
    while bit < lax.axis_size("obj"):
        steps.append(("obj", bit))
        bit *= 2
    bit = 2
    while bit < lax.axis_size("dp"):
        steps.append(("dp", bit))
        bit *= 2
    return steps


def upper_of(axis, bit):
    return (lax.axis_index(axis) // bit) % 2


def halve(values, axis, bit):
    rows = values.shape[0] // 2
    upper = upper_of(axis, bit)
    keep = lax.dynamic_slice_in_dim(values, upper * rows, rows, 0)
    send = lax.dynamic_slice_in_dim(values, (1 - upper) * rows, rows, 0)
    return keep, send


def sum_to_share(keep, send):
    for index, (axis, bit) in enumerate(exchange_steps()):
        if index > 0:
            keep, send = halve(values, axis, bit)
        got = swap_bit(send.astype(jnp.bfloat16), axis, bit)
        values = keep + got.astype(keep.dtype)
    got = swap_bit(values, "dp", 1)
    return values + got


def in_order(upper, own, other):
    place = jnp.arange(2, dtype=jnp.int32).reshape(2, 1, 1)
    both = jnp.where(place == upper, own[None], other[None])
    return both.reshape(2 * own.shape[0], own.shape[1])


def own_share(values):
    for axis, bit in exchange_steps():
        values = halve(values, axis, bit)[0]
    return values


def join_shares(values):
    steps = exchange_steps()
    for index in range(len(steps) - 1, -1, -1):
        axis, bit = steps[index]
        got = swap_bit(values, axis, bit)
        if index == 0:
            return values, got
        values = in_order(upper_of(axis, bit), values, got)


def fold_rims(current, grad, rim_outer, rim_inner, half):
    tile_rows, tile_cols = current.shape[1:]
    odd = lax.axis_index("obj") % 2 == 1
    outer, inner = swap_both(rim_outer, rim_inner, "obj")
    left, right = pick(odd, inner, outer)
    wide = jnp.zeros((2, grad.shape[1], tile_cols - 2 * half), left.dtype)
    total = grad + jnp.concatenate([left, wide, right], axis=2).astype(jnp.float32)
    low = total.astype(jnp.bfloat16)
    first, last = low[:, :half], low[:, -half:]
    above, below = shift_both(first, last, "dp")
    tall = jnp.zeros((2, tile_rows - 2 * half, tile_cols), above.dtype)
    rows = jnp.concatenate([above, tall, below], axis=1).astype(jnp.float32)
    current = current + (total[:, half : half + tile_rows] + rows)
    return current, current.astype(jnp.bfloat16)


def gather_rims(tile, half):
    low = lambda values: values.astype(jnp.bfloat16)
    above, below = shift_both(low(tile[:, :half]), low(tile[:, -half:]), "dp")
    tile = low(tile)
    first = jnp.concatenate([above[:, :, :half], tile[:, :, :half], below[:, :, :half]], axis=1)
    last = jnp.concatenate([above[:, :, -half:], tile[:, :, -half:], below[:, :, -half:]], axis=1)
    odd = lax.axis_index("obj") % 2 == 1
    outer, inner = swap_both(*pick(odd, last, first), "obj")
    return tile, above, below, outer, inner


def shards(object_field, probe_modes, amplitude, offsets):
    modes, _, side, _ = probe_modes.shape
    half = side // 2
    tile_rows = object_field.shape[1]
    tile_cols = object_field.shape[2]
    count = offsets.shape[0]
    devices = lax.axis_size("dp") * lax.axis_size("obj")
    total_positions = count * devices
    tables = split_tables(side)
    amplitude = even_odd(amplitude)
    top_rows = offsets[:, 0] - lax.axis_index("dp") * tile_rows + half
    left_cols = offsets[:, 1] - lax.axis_index("obj") * tile_cols + half
    upper = upper_of("obj", 1)
    flags = jnp.stack([lax.axis_index("obj") % 2, upper])
    split = (modes // 2, 2, side, side)
    current = object_field
    probe_parts = [
        half_modes.astype(jnp.bfloat16).reshape(split)
        for half_modes in halve(probe_modes.reshape(-1, side), "obj", 1)
    ]
    probe_share = own_share(probe_modes.reshape(-1, side))
    pieces = gather_rims(current, half)
    for turn in range(ITERS):
        grad, rim_outer, rim_inner, keep, send = propagate(
            top_rows, left_cols, flags, pieces, probe_parts, amplitude, tables
        )
        current, low_tile = fold_rims(current, grad, rim_outer, rim_inner, half)
        summed = sum_to_share(keep.reshape(-1, side), send.reshape(-1, side))
        probe_share = probe_share + summed / total_positions
        if turn + 1 < ITERS:
            pieces = gather_rims(low_tile, half)
            low_share = probe_share.astype(jnp.bfloat16)
            parts = join_shares(low_share)
            probe_parts = [part.reshape(split) for part in parts]
        else:
            rest = (probe_share - low_share.astype(jnp.float32)).astype(jnp.bfloat16)
            parts = [
                part.astype(jnp.float32) + more.astype(jnp.float32)
                for part, more in zip(parts, join_shares(rest))
            ]
            probe = in_order(upper, *parts).reshape(probe_modes.shape)
    return (current, probe)


def solution(mesh):
    in_specs = (P(None, "dp", "obj"), P(), P(("dp", "obj"), None, None), P(("dp", "obj"), None))
    out_specs = (P(None, "dp", "obj"), P())
    return jax.shard_map(shards, mesh=mesh, in_specs=in_specs, out_specs=out_specs, check_vma=False)
```

```python
import jax
import jax.numpy as jnp
import numpy as np
from jax import lax
from jax.experimental import pallas as pl
from jax.experimental.pallas import tpu as pltpu
from jax.sharding import PartitionSpec as P


ITERS = 2


EPSILON = 1e-06


LANES = 128


def swap_bit(values, axis, bit):
    return lax.ppermute(values, axis, [(i, i ^ bit) for i in range(lax.axis_size(axis))])


def shift_both(before, after, axis):
    up = [(i, i + 1) for i in range(lax.axis_size(axis) - 1)]
    previous = lax.ppermute(after, axis, up)
    following = lax.ppermute(before, axis, [(target, source) for source, target in up])
    return previous, following


def swap_both(outer, inner, axis):
    count = lax.axis_size(axis)
    inner_pairs = [(i, i ^ 1) for i in range(count)]
    outer_pairs = [(i, i + 1) for i in range(1, count - 1, 2)]
    outer_pairs = outer_pairs + [(target, source) for source, target in outer_pairs]
    outer = lax.ppermute(outer, axis, outer_pairs)
    inner = lax.ppermute(inner, axis, inner_pairs)
    return outer, inner


def pick(condition, first, second):
    return jnp.where(condition, first, second), jnp.where(condition, second, first)


def dft_tables(length):
    counter = np.arange(length, dtype=np.int32)
    phase_steps = counter[:, None] * counter[None, :] % length
    angle_grid = phase_steps.astype(np.float32) * np.float32(2.0 * np.pi / length)
    norm_factor = np.float32(1.0) / np.sqrt(np.float32(length))
    return (np.cos(angle_grid) * norm_factor, -np.sin(angle_grid) * norm_factor)


def split_tables(length):
    real_table, imag_table = dft_tables(length)
    half = length // 2
    lefts = []
    for first in (0, 1):
        re = real_table[first::2, :half]
        im = imag_table[first::2, :half]
        lefts.append(np.block([[re, -im], [im, re]]))
    return jnp.asarray(np.stack(lefts + [lefts[0].T, lefts[1].T]), jnp.bfloat16)


def even_odd(values):
    side = values.shape[-1]
    order = np.concatenate([np.arange(0, side, 2), np.arange(1, side, 2)])
    pick = jnp.asarray(np.arange(side)[:, None] == order[None, :], jnp.float32)
    right = jnp.einsum(
        "brc,ck->brk", values, pick, precision=lax.Precision.HIGHEST,
        preferred_element_type=jnp.float32,
    )
    return jnp.einsum(
        "rk,brc->bkc", pick, right, precision=lax.Precision.HIGHEST,
        preferred_element_type=jnp.float32,
    )


def mm(left, right):
    return jnp.dot(left, right, preferred_element_type=jnp.float32)


def take_patch(ext_ref, patch_ref, row, col):
    side = patch_ref.shape[1]
    width = side // LANES
    tile0 = col // LANES
    lane0 = col % LANES
    shift = (LANES - lane0) % LANES
    lane = lax.broadcasted_iota(jnp.int32, (side, LANES), 1)
    inside = lane < LANES - lane0
    for part in range(2):
        rolled = [
            pltpu.roll(ext_ref[part, tile0 + j, pl.ds(row, side), :], shift, 1)
            for j in range(width + 1)
        ]
        for j in range(width):
            patch_ref[part, :, j * LANES : (j + 1) * LANES] = jnp.where(
                inside, rolled[j], rolled[j + 1]
            )


def add_window(acc_ref, window_ref, row, col, scale):
    side = window_ref.shape[1]
    width = side // LANES
    tile0 = col // LANES
    lane0 = col % LANES
    lane = lax.broadcasted_iota(jnp.int32, (side, LANES), 1)
    inside = lane >= lane0
    zero = jnp.zeros((side, LANES), jnp.float32)
    for part in range(2):
        rolled = [
            pltpu.roll(window_ref[part, :, j * LANES : (j + 1) * LANES] * scale, lane0, 1)
            for j in range(width)
        ]
        for j in range(width + 1):
            above = rolled[j] if j < width else zero
            below = rolled[j - 1] if j > 0 else zero
            acc_ref[part, tile0 + j, pl.ds(row, side), :] += jnp.where(inside, above, below)


def propagate_body(
    rows_ref, cols_ref, flag_ref, tile_ref, above_ref, below_ref, outer_ref, inner_ref, own_ref,
    other_ref, amp_ref, table_ref, grad_ref, rim_outer_ref, rim_inner_ref, keep_ref, send_ref,
    ext_f32, patch_ref, next_ref, window_ref, acc_ref, probe_ref, probe_acc, low_ref, wide_ref,
    far_ref, ratio_ref, scale_ref,
):
    modes, _, side, _ = probe_ref.shape
    half = side // 2
    step = pl.program_id(0)
    count = pl.num_programs(0)
    tiles = ext_f32.shape[1]
    edge = half // LANES
    tile_rows = tile_ref.shape[1]
    odd = flag_ref[0]
    upper = flag_ref[1]
    share = modes // 2
    f32 = jnp.float32
    bf16 = jnp.bfloat16

    @pl.when(step == 0)
    def _():
        probe_ref[pl.ds(upper * share, share)] = own_ref[...].astype(f32)
        probe_ref[pl.ds((1 - upper) * share, share)] = other_ref[...].astype(f32)
        for part in range(2):
            for tile in range(edge):
                at = slice(tile * LANES, (tile + 1) * LANES)
                last = (tiles - edge) * odd + tile
                first = (tiles - edge) * (1 - odd) + tile
                ext_f32[part, last] = outer_ref[part, :, at].astype(f32)
                ext_f32[part, first] = inner_ref[part, :, at].astype(f32)
            for tile in range(edge, tiles - edge):
                at = slice((tile - edge) * LANES, (tile - edge + 1) * LANES)
                ext_f32[part, tile, :half] = above_ref[part, :, at].astype(f32)
                ext_f32[part, tile, half : half + tile_rows] = tile_ref[part, :, at].astype(f32)
                ext_f32[part, tile, half + tile_rows :] = below_ref[part, :, at].astype(f32)
        acc_ref[...] = jnp.zeros(acc_ref.shape, f32)
        probe_acc[...] = jnp.zeros(probe_acc.shape, f32)
        window_ref[...] = jnp.zeros(window_ref.shape, f32)
        power = jnp.zeros((side, side), f32)
        for mode in range(modes):
            for part in range(2):
                values = probe_ref[mode, part]
                power += values * values
        scale_ref[0] = 1.0 / (jnp.max(power) + EPSILON)
        take_patch(ext_f32, next_ref, rows_ref[0], cols_ref[0])

    before = jnp.maximum(step - 1, 0)
    add_window(acc_ref, window_ref, rows_ref[before], cols_ref[before], scale_ref[0])
    patch_ref[...] = next_ref[...]

    chunk = 16
    table_le = table_ref[0]
    table_lo = table_ref[1]
    table_re = table_ref[2]
    table_ro = table_ref[3]

    def make_waves(mode):
        for first in range(0, half, chunk):
            wave = []
            for rows in (slice(first, first + chunk), slice(half + first, half + first + chunk)):
                qr = probe_ref[mode, 0, rows, :]
                qi = probe_ref[mode, 1, rows, :]
                pr = patch_ref[0, rows, :]
                pi = patch_ref[1, rows, :]
                wave.append((qr * pr - qi * pi, qr * pi + qi * pr))
            for part in range(2):
                rows = slice(part * half + first, part * half + first + chunk)
                low_ref[mode, 0, rows, :] = (wave[0][part] + wave[1][part]).astype(bf16)
                low_ref[mode, 1, rows, :] = (wave[0][part] - wave[1][part]).astype(bf16)

    def left(mode):
        wide_ref[mode, 0] = mm(table_le, low_ref[mode, 0])
        wide_ref[mode, 1] = mm(table_lo, low_ref[mode, 1])

    def split_columns(mode):
        for index in range(2):
            for first in range(0, half, chunk):
                rows = slice(index * half + first, index * half + first + chunk)
                for part in range(2):
                    source = slice(part * half + first, part * half + first + chunk)
                    at = slice(part * half, (part + 1) * half)
                    near = wide_ref[mode, index, source, :half]
                    far = wide_ref[mode, index, source, half:]
                    low_ref[mode, 2, rows, at] = (near + far).astype(bf16)
                    low_ref[mode, 3, rows, at] = (near - far).astype(bf16)

    def right(mode):
        far_ref[mode, 0] = mm(low_ref[mode, 2], table_re)
        far_ref[mode, 1] = mm(low_ref[mode, 3], table_ro)

    def make_ratio():
        for index in range(2):
            for first in range(0, side, chunk):
                rows = slice(first, first + chunk)
                power = jnp.zeros((chunk, half), f32)
                for mode in range(modes):
                    re = far_ref[mode, index, rows, :half]
                    im = far_ref[mode, index, rows, half:]
                    power += re * re + im * im
                at = slice(index * half, (index + 1) * half)
                ratio_ref[rows, at] = (
                    amp_ref[0, rows, at] * lax.rsqrt(jnp.maximum(power, 1.0)) - 1.0
                )

    def make_diffs(mode):
        for index in range(2):
            for first in range(0, side, chunk):
                rows = slice(first, first + chunk)
                ratio = ratio_ref[rows, index * half : (index + 1) * half]
                for part in range(2):
                    at = slice(part * half, (part + 1) * half)
                    low_ref[mode, index, rows, at] = (
                        far_ref[mode, index, rows, at] * ratio
                    ).astype(bf16)

    def right_back(mode):
        wide_ref[mode, 0] = mm(low_ref[mode, 0], table_le)
        wide_ref[mode, 1] = mm(low_ref[mode, 1], table_lo)

    def join_columns(mode):
        for index in range(2):
            for first in range(0, half, chunk):
                source = slice(index * half + first, index * half + first + chunk)
                for part in range(2):
                    at = slice(part * half, (part + 1) * half)
                    rows = slice(part * half + first, part * half + first + chunk)
                    u = wide_ref[mode, 0, source, at]
                    v = wide_ref[mode, 1, source, at]
                    low_ref[mode, 2 + index, rows, :half] = (u + v).astype(bf16)
                    low_ref[mode, 2 + index, rows, half:] = (u - v).astype(bf16)

    def left_back(mode):
        far_ref[mode, 0] = mm(table_re, low_ref[mode, 2])
        far_ref[mode, 1] = mm(table_ro, low_ref[mode, 3])

    def gather_terms(mode):
        for first in range(0, half, 8):
            even_re = far_ref[mode, 0, first : first + 8, :]
            odd_re = far_ref[mode, 1, first : first + 8, :]
            even_im = far_ref[mode, 0, half + first : half + first + 8, :]
            odd_im = far_ref[mode, 1, half + first : half + first + 8, :]
            for index in range(2):
                rows = slice(index * half + first, index * half + first + 8)
                chi_re = even_re + odd_re if index == 0 else even_re - odd_re
                chi_im = even_im + odd_im if index == 0 else even_im - odd_im
                qr = probe_ref[mode, 0, rows, :]
                qi = probe_ref[mode, 1, rows, :]
                pr = patch_ref[0, rows, :]
                pi = patch_ref[1, rows, :]
                term_re = qr * chi_re + qi * chi_im
                term_im = qr * chi_im - qi * chi_re
                if mode > 0:
                    term_re += window_ref[0, rows, :]
                    term_im += window_ref[1, rows, :]
                window_ref[0, rows, :] = term_re
                window_ref[1, rows, :] = term_im
                probe_acc[mode, 0, rows, :] += pr * chi_re + pi * chi_im
                probe_acc[mode, 1, rows, :] += pr * chi_im - pi * chi_re

    for pair in range(0, modes, 2):
        make_waves(pair)
        left(pair)
        make_waves(pair + 1)
        left(pair + 1)
        split_columns(pair)
        right(pair)
        split_columns(pair + 1)
        right(pair + 1)
    make_ratio()
    for pair in range(0, modes, 2):
        make_diffs(pair)
        right_back(pair)
        make_diffs(pair + 1)
        right_back(pair + 1)
        if pair > 0:
            gather_terms(pair - 2)
        join_columns(pair)
        left_back(pair)
        join_columns(pair + 1)
        left_back(pair + 1)
        if pair > 0:
            gather_terms(pair - 1)
    gather_terms(modes - 2)
    gather_terms(modes - 1)

    after = jnp.minimum(step + 1, count - 1)
    take_patch(ext_f32, next_ref, rows_ref[after], cols_ref[after])

    @pl.when(step == count - 1)
    def _():
        add_window(acc_ref, window_ref, rows_ref[step], cols_ref[step], scale_ref[0])
        keep_ref[...] = probe_acc[pl.ds(upper * share, share)]
        send_ref[...] = probe_acc[pl.ds((1 - upper) * share, share)].astype(send_ref.dtype)
        for part in range(2):
            for tile in range(edge):
                at = slice(tile * LANES, (tile + 1) * LANES)
                last = (tiles - edge) * odd + tile
                first = (tiles - edge) * (1 - odd) + tile
                rim_outer_ref[part, :, at] = acc_ref[part, last].astype(rim_outer_ref.dtype)
                rim_inner_ref[part, :, at] = acc_ref[part, first].astype(rim_inner_ref.dtype)
            for tile in range(edge, tiles - edge):
                at = slice((tile - edge) * LANES, (tile - edge + 1) * LANES)
                grad_ref[part, :, at] = acc_ref[part, tile]


def propagate(rows, cols, flags, pieces, probe_parts, amplitude, tables):
    count = rows.shape[0]
    share, _, side, _ = probe_parts[0].shape
    modes = 2 * share
    half = side // 2
    tile_rows, tile_cols = pieces[0].shape[1:]
    ext_rows = tile_rows + side
    tiles = (tile_cols + side) // LANES

    def whole(*shape):
        return pl.BlockSpec(
            shape, lambda i, *_: (0,) * len(shape), pipeline_mode=pl.Buffered(1)
        )

    outs = (
        jax.ShapeDtypeStruct((2, ext_rows, tile_cols), jnp.float32),
        jax.ShapeDtypeStruct((2, ext_rows, half), jnp.bfloat16),
        jax.ShapeDtypeStruct((2, ext_rows, half), jnp.bfloat16),
        jax.ShapeDtypeStruct((share, 2, side, side), jnp.float32),
        jax.ShapeDtypeStruct((share, 2, side, side), jnp.bfloat16),
    )
    return pl.pallas_call(
        propagate_body,
        out_shape=outs,
        grid_spec=pltpu.PrefetchScalarGridSpec(
            num_scalar_prefetch=3,
            grid=(count,),
            in_specs=[whole(*piece.shape) for piece in pieces]
            + [whole(*part.shape) for part in probe_parts]
            + [
                pl.BlockSpec((1, side, side), lambda i, *_: (i, 0, 0)),
                whole(*tables.shape),
            ],
            out_specs=tuple(whole(*out.shape) for out in outs),
            scratch_shapes=[
                pltpu.VMEM((2, tiles, ext_rows, LANES), jnp.float32),
                pltpu.VMEM((2, side, side), jnp.float32),
                pltpu.VMEM((2, side, side), jnp.float32),
                pltpu.VMEM((2, side, side), jnp.float32),
                pltpu.VMEM((2, tiles, ext_rows, LANES), jnp.float32),
                pltpu.VMEM((modes, 2, side, side), jnp.float32),
                pltpu.VMEM((modes, 2, side, side), jnp.float32),
                pltpu.VMEM((modes, 4, side, side), jnp.bfloat16),
                pltpu.VMEM((modes, 2, side, side), jnp.float32),
                pltpu.VMEM((modes, 2, side, side), jnp.float32),
                pltpu.VMEM((side, side), jnp.float32),
                pltpu.SMEM((1,), jnp.float32),
            ],
        ),
        name="propagate",
    )(rows, cols, flags, *pieces, *probe_parts, amplitude, tables)


def exchange_steps():
    steps = []
    bit = 1
    while bit < lax.axis_size("obj"):
        steps.append(("obj", bit))
        bit *= 2
    bit = 2
    while bit < lax.axis_size("dp"):
        steps.append(("dp", bit))
        bit *= 2
    return steps


def upper_of(axis, bit):
    return (lax.axis_index(axis) // bit) % 2


def halve(values, axis, bit):
    rows = values.shape[0] // 2
    upper = upper_of(axis, bit)
    keep = lax.dynamic_slice_in_dim(values, upper * rows, rows, 0)
    send = lax.dynamic_slice_in_dim(values, (1 - upper) * rows, rows, 0)
    return keep, send


def sum_to_share(keep, send):
    for index, (axis, bit) in enumerate(exchange_steps()):
        if index > 0:
            keep, send = halve(values, axis, bit)
        got = swap_bit(send.astype(jnp.bfloat16), axis, bit)
        values = keep + got.astype(keep.dtype)
    got = swap_bit(values, "dp", 1)
    return values + got


def in_order(upper, own, other):
    place = jnp.arange(2, dtype=jnp.int32).reshape(2, 1, 1)
    both = jnp.where(place == upper, own[None], other[None])
    return both.reshape(2 * own.shape[0], own.shape[1])


def own_share(values):
    for axis, bit in exchange_steps():
        values = halve(values, axis, bit)[0]
    return values


def join_shares(values):
    steps = exchange_steps()
    for index in range(len(steps) - 1, -1, -1):
        axis, bit = steps[index]
        got = swap_bit(values, axis, bit)
        if index == 0:
            return values, got
        values = in_order(upper_of(axis, bit), values, got)


def fold_rims(current, grad, rim_outer, rim_inner, half):
    tile_rows, tile_cols = current.shape[1:]
    odd = lax.axis_index("obj") % 2 == 1
    outer, inner = swap_both(rim_outer, rim_inner, "obj")
    left, right = pick(odd, inner, outer)
    wide = jnp.zeros((2, grad.shape[1], tile_cols - 2 * half), left.dtype)
    total = grad + jnp.concatenate([left, wide, right], axis=2).astype(jnp.float32)
    low = total.astype(jnp.bfloat16)
    first, last = low[:, :half], low[:, -half:]
    above, below = shift_both(first, last, "dp")
    tall = jnp.zeros((2, tile_rows - 2 * half, tile_cols), above.dtype)
    rows = jnp.concatenate([above, tall, below], axis=1).astype(jnp.float32)
    current = current + (total[:, half : half + tile_rows] + rows)
    return current, current.astype(jnp.bfloat16)


def gather_rims(tile, half):
    low = lambda values: values.astype(jnp.bfloat16)
    above, below = shift_both(low(tile[:, :half]), low(tile[:, -half:]), "dp")
    tile = low(tile)
    first = jnp.concatenate([above[:, :, :half], tile[:, :, :half], below[:, :, :half]], axis=1)
    last = jnp.concatenate([above[:, :, -half:], tile[:, :, -half:], below[:, :, -half:]], axis=1)
    odd = lax.axis_index("obj") % 2 == 1
    outer, inner = swap_both(*pick(odd, last, first), "obj")
    return tile, above, below, outer, inner


def shards(object_field, probe_modes, amplitude, offsets):
    modes, _, side, _ = probe_modes.shape
    half = side // 2
    tile_rows = object_field.shape[1]
    tile_cols = object_field.shape[2]
    count = offsets.shape[0]
    devices = lax.axis_size("dp") * lax.axis_size("obj")
    total_positions = count * devices
    tables = split_tables(side)
    amplitude = even_odd(amplitude)
    top_rows = offsets[:, 0] - lax.axis_index("dp") * tile_rows + half
    left_cols = offsets[:, 1] - lax.axis_index("obj") * tile_cols + half
    upper = upper_of("obj", 1)
    flags = jnp.stack([lax.axis_index("obj") % 2, upper])
    split = (modes // 2, 2, side, side)
    current = object_field
    probe_parts = [
        half_modes.astype(jnp.bfloat16).reshape(split)
        for half_modes in halve(probe_modes.reshape(-1, side), "obj", 1)
    ]
    probe_share = own_share(probe_modes.reshape(-1, side))
    pieces = gather_rims(current, half)
    for turn in range(ITERS):
        grad, rim_outer, rim_inner, keep, send = propagate(
            top_rows, left_cols, flags, pieces, probe_parts, amplitude, tables
        )
        current, low_tile = fold_rims(current, grad, rim_outer, rim_inner, half)
        summed = sum_to_share(keep.reshape(-1, side), send.reshape(-1, side))
        probe_share = probe_share + summed / total_positions
        if turn + 1 < ITERS:
            pieces = gather_rims(low_tile, half)
            low_share = probe_share.astype(jnp.bfloat16)
            parts = join_shares(low_share)
            probe_parts = [part.reshape(split) for part in parts]
        else:
            rest = (probe_share - low_share.astype(jnp.float32)).astype(jnp.bfloat16)
            rests = join_shares(rest)
            low = in_order(upper, *parts).astype(jnp.float32)
            probe = low + in_order(upper, *rests).astype(jnp.float32)
            probe = probe.reshape(probe_modes.shape)
    return (current, probe)


def solution(mesh):
    in_specs = (P(None, "dp", "obj"), P(), P(("dp", "obj"), None, None), P(("dp", "obj"), None))
    out_specs = (P(None, "dp", "obj"), P())
    return jax.shard_map(shards, mesh=mesh, in_specs=in_specs, out_specs=out_specs, check_vma=False)
```

```python
import jax
import jax.numpy as jnp
import numpy as np
from jax import lax
from jax.experimental import pallas as pl
from jax.experimental.pallas import tpu as pltpu
from jax.sharding import PartitionSpec as P


ITERS = 2


EPSILON = 1e-06


LANES = 128


def swap_bit(values, axis, bit):
    return lax.ppermute(values, axis, [(i, i ^ bit) for i in range(lax.axis_size(axis))])


def shift_both(before, after, axis):
    up = [(i, i + 1) for i in range(lax.axis_size(axis) - 1)]
    previous = lax.ppermute(after, axis, up)
    following = lax.ppermute(before, axis, [(target, source) for source, target in up])
    return previous, following


def swap_both(outer, inner, axis):
    count = lax.axis_size(axis)
    inner_pairs = [(i, i ^ 1) for i in range(count)]
    outer_pairs = [(i, i + 1) for i in range(1, count - 1, 2)]
    outer_pairs = outer_pairs + [(target, source) for source, target in outer_pairs]
    outer = lax.ppermute(outer, axis, outer_pairs)
    inner = lax.ppermute(inner, axis, inner_pairs)
    return outer, inner


def pick(condition, first, second):
    return jnp.where(condition, first, second), jnp.where(condition, second, first)


def dft_tables(length):
    counter = np.arange(length, dtype=np.int32)
    phase_steps = counter[:, None] * counter[None, :] % length
    angle_grid = phase_steps.astype(np.float32) * np.float32(2.0 * np.pi / length)
    norm_factor = np.float32(1.0) / np.sqrt(np.float32(length))
    return (np.cos(angle_grid) * norm_factor, -np.sin(angle_grid) * norm_factor)


def split_tables(length):
    real_table, imag_table = dft_tables(length)
    half = length // 2
    lefts = []
    for first in (0, 1):
        re = real_table[first::2, :half]
        im = imag_table[first::2, :half]
        lefts.append(np.block([[re, -im], [im, re]]))
    return jnp.asarray(np.stack(lefts + [lefts[0].T, lefts[1].T]), jnp.bfloat16)


def even_odd(values):
    side = values.shape[-1]
    order = np.concatenate([np.arange(0, side, 2), np.arange(1, side, 2)])
    pick = jnp.asarray(np.arange(side)[:, None] == order[None, :], jnp.float32)
    right = jnp.einsum(
        "brc,ck->brk", values, pick, precision=lax.Precision.HIGHEST,
        preferred_element_type=jnp.float32,
    )
    return jnp.einsum(
        "rk,brc->bkc", pick, right, precision=lax.Precision.HIGHEST,
        preferred_element_type=jnp.float32,
    )


def mm(left, right):
    return jnp.dot(left, right, preferred_element_type=jnp.float32)


def take_patch(ext_ref, patch_ref, slot, row, col):
    side = patch_ref.shape[2]
    width = side // LANES
    tile0 = col // LANES
    lane0 = col % LANES
    shift = (LANES - lane0) % LANES
    lane = lax.broadcasted_iota(jnp.int32, (side, LANES), 1)
    inside = lane < LANES - lane0
    for part in range(2):
        rolled = [
            pltpu.roll(ext_ref[part, tile0 + j, pl.ds(row, side), :], shift, 1)
            for j in range(width + 1)
        ]
        for j in range(width):
            patch_ref[slot, part, :, j * LANES : (j + 1) * LANES] = jnp.where(
                inside, rolled[j], rolled[j + 1]
            )


def add_window(acc_ref, window_ref, row, col, scale):
    side = window_ref.shape[1]
    width = side // LANES
    tile0 = col // LANES
    lane0 = col % LANES
    lane = lax.broadcasted_iota(jnp.int32, (side, LANES), 1)
    inside = lane >= lane0
    zero = jnp.zeros((side, LANES), jnp.float32)
    for part in range(2):
        rolled = [
            pltpu.roll(window_ref[part, :, j * LANES : (j + 1) * LANES] * scale, lane0, 1)
            for j in range(width)
        ]
        for j in range(width + 1):
            above = rolled[j] if j < width else zero
            below = rolled[j - 1] if j > 0 else zero
            acc_ref[part, tile0 + j, pl.ds(row, side), :] += jnp.where(inside, above, below)


def propagate_body(
    rows_ref, cols_ref, flag_ref, tile_ref, above_ref, below_ref, outer_ref, inner_ref, own_ref,
    other_ref, amp_ref, table_ref, grad_ref, rim_outer_ref, rim_inner_ref, keep_ref, send_ref,
    ext_f32, patch_ref, window_ref, acc_ref, probe_ref, probe_acc, low_ref, wide_ref,
    far_ref, ratio_ref, scale_ref,
):
    modes, _, side, _ = probe_ref.shape
    half = side // 2
    step = pl.program_id(0)
    count = pl.num_programs(0)
    tiles = ext_f32.shape[1]
    edge = half // LANES
    tile_rows = tile_ref.shape[1]
    odd = flag_ref[0]
    upper = flag_ref[1]
    share = modes // 2
    f32 = jnp.float32
    bf16 = jnp.bfloat16

    @pl.when(step == 0)
    def _():
        probe_ref[pl.ds(upper * share, share)] = own_ref[...].astype(f32)
        probe_ref[pl.ds((1 - upper) * share, share)] = other_ref[...].astype(f32)
        for part in range(2):
            for tile in range(edge):
                at = slice(tile * LANES, (tile + 1) * LANES)
                last = (tiles - edge) * odd + tile
                first = (tiles - edge) * (1 - odd) + tile
                ext_f32[part, last] = outer_ref[part, :, at].astype(f32)
                ext_f32[part, first] = inner_ref[part, :, at].astype(f32)
            for tile in range(edge, tiles - edge):
                at = slice((tile - edge) * LANES, (tile - edge + 1) * LANES)
                ext_f32[part, tile, :half] = above_ref[part, :, at].astype(f32)
                ext_f32[part, tile, half : half + tile_rows] = tile_ref[part, :, at].astype(f32)
                ext_f32[part, tile, half + tile_rows :] = below_ref[part, :, at].astype(f32)
        acc_ref[...] = jnp.zeros(acc_ref.shape, f32)
        probe_acc[...] = jnp.zeros(probe_acc.shape, f32)
        window_ref[...] = jnp.zeros(window_ref.shape, f32)
        power = jnp.zeros((side, side), f32)
        for mode in range(modes):
            for part in range(2):
                values = probe_ref[mode, part]
                power += values * values
        scale_ref[0] = 1.0 / (jnp.max(power) + EPSILON)
        take_patch(ext_f32, patch_ref, 0, rows_ref[0], cols_ref[0])

    before = jnp.maximum(step - 1, 0)
    add_window(acc_ref, window_ref, rows_ref[before], cols_ref[before], scale_ref[0])
    now = step % 2

    chunk = 16
    table_le = table_ref[0]
    table_lo = table_ref[1]
    table_re = table_ref[2]
    table_ro = table_ref[3]

    def make_waves(group):
        for first in range(0, half, chunk):
            halves = (slice(first, first + chunk), slice(half + first, half + first + chunk))
            patch = [(patch_ref[now, 0, rows, :], patch_ref[now, 1, rows, :]) for rows in halves]
            for mode in group:
                wave = []
                for rows, (pr, pi) in zip(halves, patch):
                    qr = probe_ref[mode, 0, rows, :]
                    qi = probe_ref[mode, 1, rows, :]
                    wave.append((qr * pr - qi * pi, qr * pi + qi * pr))
                for part in range(2):
                    rows = slice(part * half + first, part * half + first + chunk)
                    low_ref[mode, 0, rows, :] = (wave[0][part] + wave[1][part]).astype(bf16)
                    low_ref[mode, 1, rows, :] = (wave[0][part] - wave[1][part]).astype(bf16)

    def left(mode):
        wide_ref[mode, 0] = mm(table_le, low_ref[mode, 0])
        wide_ref[mode, 1] = mm(table_lo, low_ref[mode, 1])

    def split_columns(mode):
        for index in range(2):
            for first in range(0, half, chunk):
                rows = slice(index * half + first, index * half + first + chunk)
                for part in range(2):
                    source = slice(part * half + first, part * half + first + chunk)
                    at = slice(part * half, (part + 1) * half)
                    near = wide_ref[mode, index, source, :half]
                    far = wide_ref[mode, index, source, half:]
                    low_ref[mode, 2, rows, at] = (near + far).astype(bf16)
                    low_ref[mode, 3, rows, at] = (near - far).astype(bf16)

    def right(mode):
        far_ref[mode, 0] = mm(low_ref[mode, 2], table_re)
        far_ref[mode, 1] = mm(low_ref[mode, 3], table_ro)

    def make_ratio():
        for index in range(2):
            for first in range(0, side, chunk):
                rows = slice(first, first + chunk)
                power = jnp.zeros((chunk, half), f32)
                for mode in range(modes):
                    re = far_ref[mode, index, rows, :half]
                    im = far_ref[mode, index, rows, half:]
                    power += re * re + im * im
                at = slice(index * half, (index + 1) * half)
                ratio_ref[rows, at] = (
                    amp_ref[0, rows, at] * lax.rsqrt(jnp.maximum(power, 1.0)) - 1.0
                )

    def make_diffs(mode):
        for index in range(2):
            for first in range(0, side, chunk):
                rows = slice(first, first + chunk)
                ratio = ratio_ref[rows, index * half : (index + 1) * half]
                for part in range(2):
                    at = slice(part * half, (part + 1) * half)
                    low_ref[mode, index, rows, at] = (
                        far_ref[mode, index, rows, at] * ratio
                    ).astype(bf16)

    def right_back(mode):
        wide_ref[mode, 0] = mm(low_ref[mode, 0], table_le)
        wide_ref[mode, 1] = mm(low_ref[mode, 1], table_lo)

    def join_columns(mode):
        for index in range(2):
            for first in range(0, half, chunk):
                source = slice(index * half + first, index * half + first + chunk)
                for part in range(2):
                    at = slice(part * half, (part + 1) * half)
                    rows = slice(part * half + first, part * half + first + chunk)
                    u = wide_ref[mode, 0, source, at]
                    v = wide_ref[mode, 1, source, at]
                    low_ref[mode, 2 + index, rows, :half] = (u + v).astype(bf16)
                    low_ref[mode, 2 + index, rows, half:] = (u - v).astype(bf16)

    def left_back(mode):
        far_ref[mode, 0] = mm(table_re, low_ref[mode, 2])
        far_ref[mode, 1] = mm(table_ro, low_ref[mode, 3])

    def gather_terms(group):
        for first in range(0, half, 8):
            for index in range(2):
                rows = slice(index * half + first, index * half + first + 8)
                pr = patch_ref[now, 0, rows, :]
                pi = patch_ref[now, 1, rows, :]
                sum_re = window_ref[0, rows, :] if group[0] > 0 else 0.0
                sum_im = window_ref[1, rows, :] if group[0] > 0 else 0.0
                for mode in group:
                    even_re = far_ref[mode, 0, first : first + 8, :]
                    odd_re = far_ref[mode, 1, first : first + 8, :]
                    even_im = far_ref[mode, 0, half + first : half + first + 8, :]
                    odd_im = far_ref[mode, 1, half + first : half + first + 8, :]
                    chi_re = even_re + odd_re if index == 0 else even_re - odd_re
                    chi_im = even_im + odd_im if index == 0 else even_im - odd_im
                    qr = probe_ref[mode, 0, rows, :]
                    qi = probe_ref[mode, 1, rows, :]
                    sum_re += qr * chi_re + qi * chi_im
                    sum_im += qr * chi_im - qi * chi_re
                    probe_acc[mode, 0, rows, :] += pr * chi_re + pi * chi_im
                    probe_acc[mode, 1, rows, :] += pr * chi_im - pi * chi_re
                window_ref[0, rows, :] = sum_re
                window_ref[1, rows, :] = sum_im

    pairs = [(first, first + 1) for first in range(0, modes, 2)]
    make_waves(pairs[0])
    for index, (one, two) in enumerate(pairs):
        left(one)
        left(two)
        if index + 1 < len(pairs):
            make_waves(pairs[index + 1])
        split_columns(one)
        right(one)
        split_columns(two)
        right(two)
    make_ratio()
    for index, (one, two) in enumerate(pairs):
        make_diffs(one)
        right_back(one)
        make_diffs(two)
        right_back(two)
        if index > 0:
            gather_terms(pairs[index - 1])
        join_columns(one)
        left_back(one)
        join_columns(two)
        left_back(two)
    gather_terms(pairs[-1])

    after = jnp.minimum(step + 1, count - 1)
    take_patch(ext_f32, patch_ref, 1 - now, rows_ref[after], cols_ref[after])

    @pl.when(step == count - 1)
    def _():
        add_window(acc_ref, window_ref, rows_ref[step], cols_ref[step], scale_ref[0])
        keep_ref[...] = probe_acc[pl.ds(upper * share, share)]
        send_ref[...] = probe_acc[pl.ds((1 - upper) * share, share)].astype(send_ref.dtype)
        for part in range(2):
            for tile in range(edge):
                at = slice(tile * LANES, (tile + 1) * LANES)
                last = (tiles - edge) * odd + tile
                first = (tiles - edge) * (1 - odd) + tile
                rim_outer_ref[part, :, at] = acc_ref[part, last].astype(rim_outer_ref.dtype)
                rim_inner_ref[part, :, at] = acc_ref[part, first].astype(rim_inner_ref.dtype)
            for tile in range(edge, tiles - edge):
                at = slice((tile - edge) * LANES, (tile - edge + 1) * LANES)
                grad_ref[part, :, at] = acc_ref[part, tile]


def propagate(rows, cols, flags, pieces, probe_parts, amplitude, tables):
    count = rows.shape[0]
    share, _, side, _ = probe_parts[0].shape
    modes = 2 * share
    half = side // 2
    tile_rows, tile_cols = pieces[0].shape[1:]
    ext_rows = tile_rows + side
    tiles = (tile_cols + side) // LANES

    def whole(*shape):
        return pl.BlockSpec(
            shape, lambda i, *_: (0,) * len(shape), pipeline_mode=pl.Buffered(1)
        )

    outs = (
        jax.ShapeDtypeStruct((2, ext_rows, tile_cols), jnp.float32),
        jax.ShapeDtypeStruct((2, ext_rows, half), jnp.bfloat16),
        jax.ShapeDtypeStruct((2, ext_rows, half), jnp.bfloat16),
        jax.ShapeDtypeStruct((share, 2, side, side), jnp.float32),
        jax.ShapeDtypeStruct((share, 2, side, side), jnp.bfloat16),
    )
    return pl.pallas_call(
        propagate_body,
        out_shape=outs,
        grid_spec=pltpu.PrefetchScalarGridSpec(
            num_scalar_prefetch=3,
            grid=(count,),
            in_specs=[whole(*piece.shape) for piece in pieces]
            + [whole(*part.shape) for part in probe_parts]
            + [
                pl.BlockSpec((1, side, side), lambda i, *_: (i, 0, 0)),
                whole(*tables.shape),
            ],
            out_specs=tuple(whole(*out.shape) for out in outs),
            scratch_shapes=[
                pltpu.VMEM((2, tiles, ext_rows, LANES), jnp.float32),
                pltpu.VMEM((2, 2, side, side), jnp.float32),
                pltpu.VMEM((2, side, side), jnp.float32),
                pltpu.VMEM((2, tiles, ext_rows, LANES), jnp.float32),
                pltpu.VMEM((modes, 2, side, side), jnp.float32),
                pltpu.VMEM((modes, 2, side, side), jnp.float32),
                pltpu.VMEM((modes, 4, side, side), jnp.bfloat16),
                pltpu.VMEM((modes, 2, side, side), jnp.float32),
                pltpu.VMEM((modes, 2, side, side), jnp.float32),
                pltpu.VMEM((side, side), jnp.float32),
                pltpu.SMEM((1,), jnp.float32),
            ],
        ),
        name="propagate",
    )(rows, cols, flags, *pieces, *probe_parts, amplitude, tables)


def exchange_steps():
    steps = []
    bit = 1
    while bit < lax.axis_size("obj"):
        steps.append(("obj", bit))
        bit *= 2
    bit = 2
    while bit < lax.axis_size("dp"):
        steps.append(("dp", bit))
        bit *= 2
    return steps


def upper_of(axis, bit):
    return (lax.axis_index(axis) // bit) % 2


def halve(values, axis, bit):
    rows = values.shape[0] // 2
    upper = upper_of(axis, bit)
    keep = lax.dynamic_slice_in_dim(values, upper * rows, rows, 0)
    send = lax.dynamic_slice_in_dim(values, (1 - upper) * rows, rows, 0)
    return keep, send


def sum_to_share(keep, send):
    for index, (axis, bit) in enumerate(exchange_steps()):
        if index > 0:
            keep, send = halve(values, axis, bit)
        got = swap_bit(send.astype(jnp.bfloat16), axis, bit)
        values = keep + got.astype(keep.dtype)
    values = values.astype(jnp.bfloat16)
    got = swap_bit(values, "dp", 1)
    return values.astype(jnp.float32) + got.astype(jnp.float32)


def in_order(upper, own, other):
    place = jnp.arange(2, dtype=jnp.int32).reshape(2, 1, 1)
    both = jnp.where(place == upper, own[None], other[None])
    return both.reshape(2 * own.shape[0], own.shape[1])


def own_share(values):
    for axis, bit in exchange_steps():
        values = halve(values, axis, bit)[0]
    return values


def join_shares(values):
    steps = exchange_steps()
    for index in range(len(steps) - 1, -1, -1):
        axis, bit = steps[index]
        got = swap_bit(values, axis, bit)
        if index == 0:
            return values, got
        values = in_order(upper_of(axis, bit), values, got)


def fold_rims(current, grad, rim_outer, rim_inner, half):
    tile_rows, tile_cols = current.shape[1:]
    odd = lax.axis_index("obj") % 2 == 1
    outer, inner = swap_both(rim_outer, rim_inner, "obj")
    left, right = pick(odd, inner, outer)
    wide = jnp.zeros((2, grad.shape[1], tile_cols - 2 * half), left.dtype)
    total = grad + jnp.concatenate([left, wide, right], axis=2).astype(jnp.float32)
    low = total.astype(jnp.bfloat16)
    first, last = low[:, :half], low[:, -half:]
    above, below = shift_both(first, last, "dp")
    tall = jnp.zeros((2, tile_rows - 2 * half, tile_cols), above.dtype)
    rows = jnp.concatenate([above, tall, below], axis=1).astype(jnp.float32)
    current = current + (total[:, half : half + tile_rows] + rows)
    return current, current.astype(jnp.bfloat16)


def gather_rims(tile, half):
    low = lambda values: values.astype(jnp.bfloat16)
    above, below = shift_both(low(tile[:, :half]), low(tile[:, -half:]), "dp")
    tile = low(tile)
    first = jnp.concatenate([above[:, :, :half], tile[:, :, :half], below[:, :, :half]], axis=1)
    last = jnp.concatenate([above[:, :, -half:], tile[:, :, -half:], below[:, :, -half:]], axis=1)
    odd = lax.axis_index("obj") % 2 == 1
    outer, inner = swap_both(*pick(odd, last, first), "obj")
    return tile, above, below, outer, inner


def shards(object_field, probe_modes, amplitude, offsets):
    modes, _, side, _ = probe_modes.shape
    half = side // 2
    tile_rows = object_field.shape[1]
    tile_cols = object_field.shape[2]
    count = offsets.shape[0]
    devices = lax.axis_size("dp") * lax.axis_size("obj")
    total_positions = count * devices
    tables = split_tables(side)
    amplitude = even_odd(amplitude)
    top_rows = offsets[:, 0] - lax.axis_index("dp") * tile_rows + half
    left_cols = offsets[:, 1] - lax.axis_index("obj") * tile_cols + half
    upper = upper_of("obj", 1)
    flags = jnp.stack([lax.axis_index("obj") % 2, upper])
    split = (modes // 2, 2, side, side)
    current = object_field
    probe_parts = [
        half_modes.astype(jnp.bfloat16).reshape(split)
        for half_modes in halve(probe_modes.reshape(-1, side), "obj", 1)
    ]
    probe_share = own_share(probe_modes.reshape(-1, side))
    pieces = gather_rims(current, half)
    for turn in range(ITERS):
        grad, rim_outer, rim_inner, keep, send = propagate(
            top_rows, left_cols, flags, pieces, probe_parts, amplitude, tables
        )
        current, low_tile = fold_rims(current, grad, rim_outer, rim_inner, half)
        summed = sum_to_share(keep.reshape(-1, side), send.reshape(-1, side))
        probe_share = probe_share + summed / total_positions
        if turn + 1 < ITERS:
            pieces = gather_rims(low_tile, half)
            low_share = probe_share.astype(jnp.bfloat16)
            parts = join_shares(low_share)
            probe_parts = [part.reshape(split) for part in parts]
        else:
            rest = (probe_share - low_share.astype(jnp.float32)).astype(jnp.bfloat16)
            rests = join_shares(rest)
            low = in_order(upper, *parts).astype(jnp.float32)
            probe = low + in_order(upper, *rests).astype(jnp.float32)
            probe = probe.reshape(probe_modes.shape)
    return (current, probe)


def solution(mesh):
    in_specs = (P(None, "dp", "obj"), P(), P(("dp", "obj"), None, None), P(("dp", "obj"), None))
    out_specs = (P(None, "dp", "obj"), P())
    return jax.shard_map(shards, mesh=mesh, in_specs=in_specs, out_specs=out_specs, check_vma=False)
```
